512 devices in a mesh: cluster: 16 (over z, x_lo), sub: 32 (over y, x_hi, core).
Axes of the slice: x: 4 (x_hi: 2, x_lo: 2; x = x_hi * 2 + x_lo), y: 8, z: 8, core: 2. Of those that a mesh axis runs over, the one named last changes fastest.
Arguments:
- schur_block: bfloat16 [16, 32, 1024, 1024], P('cluster', 'sub'), as said below
- load_cases: float32 [16, 32, 1024, 64], P('cluster', 'sub'), may hold values from -30 to 30
- precond_scale: float32 [16, 32, 1024], P('cluster', 'sub'), may hold values from 0.5 to 2
- coarse_basis: float32 [16, 32, 6, 1024], P('cluster', 'sub'), may hold values from -1 to 1
- coarse_inverse: float32 [16, 192, 192], P('cluster', 'sub'), as said below
- corner_weight: float32 [16, 512], P('cluster', 'sub'), may hold values from 0.5 to 4
- corner_index: int32 [16, 32, 64], P('cluster', 'sub'), may hold values from 0 to 511
- iface_block: int32 [16, 32, 2], P('cluster', 'sub'), may hold values from 0 to 6
- glue_link: int32 [16, 32], P('cluster', 'sub'), may hold values 0 or 1
Outputs:
- solution: float32 [16, 32, 1024, 64], P('cluster', 'sub')
The draws below stay inside these ranges and needn't reach their ends.
Inputs may be any that keep to these rules, and one draw needn't show every extreme that they name: `schur_block`: each block is symmetric positive definite. `coarse_inverse`: each cluster's matrix is symmetric positive definite.
All inputs are finite; a program needn't handle non-finite values. No bound on the sum of `glue_link` on one device may be relied on, other than what follows from the above.
Results may differ from the reference program's by a relative error of at most 0.0007.
Values sent between devices are 32-bit elements; how exact they have to be, the bound alone decides.
A program may use at most 64 MiB of HBM per device.

```python
import math
import jax
import jax.numpy as jnp
from jax import lax

W = 1024
R = 64
NC = 64
NI = 128
NZ = 6
ITERS = 3
NCL = 16
SUBS = 32
KC = 512
NB = 7
CM = 192


def draw_schur_block(key, part):

    def one_cluster(cluster_key):
        key_noise, key_diag = jax.random.split(cluster_key)
        off_diag = jax.random.normal(key_noise, (SUBS, W, W), jnp.float32) * (0.2 / math.sqrt(W))
        diagonal = jnp.exp(jax.random.uniform(key_diag, (SUBS, W), jnp.float32, 0.0, math.log(3.0)))
        symmetric = off_diag + jnp.swapaxes(off_diag, 1, 2)
        identity_mat = jnp.eye(W, dtype=jnp.float32)
        return (symmetric + identity_mat[None, :, :] * diagonal[:, :, None]).astype(jnp.bfloat16)
    cluster_keys = jax.random.split(key, NCL)
    return lax.map(one_cluster, cluster_keys)


def draw_load_cases(key, part):
    key_base, key_rows = jax.random.split(key, 2)
    cluster_ramp = 1.0 + 2.0 * jnp.arange(NCL, dtype=jnp.float32) / max(NCL - 1, 1)
    normal_part = jax.random.normal(key_base, (NCL, SUBS, W, R), jnp.float32)
    row_scale = jnp.exp(jax.random.uniform(key_rows, (NCL, SUBS, W, 1), jnp.float32, 0.0, math.log(4.0)))
    return jnp.clip(normal_part * row_scale * cluster_ramp[:, None, None, None], -30.0, 30.0)


def draw_coarse_inverse(key, part):
    key_noise, key_diag = jax.random.split(key)
    off_diag = jax.random.normal(key_noise, (NCL, CM, CM), jnp.float32) * (0.14 / math.sqrt(CM))
    diagonal = jax.random.uniform(key_diag, (NCL, CM), jnp.float32, 0.5, 1.0)
    symmetric = off_diag + jnp.swapaxes(off_diag, 1, 2)
    identity_mat = jnp.eye(CM, dtype=jnp.float32)
    return symmetric + identity_mat[None, :, :] * diagonal[:, :, None]


def with_ends(drawn, stream_key, low, high):
    shape = drawn.shape
    spot = [jax.random.randint(jax.random.fold_in(stream_key, axis), (), 0, shape[axis]) for axis in range(len(shape))]
    drawn = drawn.at[tuple(spot)].set(low)
    longest = shape.index(max(shape))
    spot[longest] = (spot[longest] + 1) % shape[longest]
    return drawn.at[tuple(spot)].set(high)


def steps_of(rng, dims, shards, low, high):
    def one(dim, parts):
        steps = jax.random.uniform(jax.random.fold_in(jax.random.fold_in(rng, 6), dim), (parts,), jnp.float32, low / len(shards), high / len(shards))
        return jnp.repeat(jnp.exp(steps), dims[dim] // parts).reshape((-1,) + (1,) * (len(dims) - dim - 1))

    loudness = one(*shards[0])
    for cut in shards[1:]:
        loudness = loudness * one(*cut)
    return loudness


def noise(own_key, extent, width, limit, cuts=(), held_as=jnp.bfloat16):
    values = width * jax.random.normal(own_key, extent, jnp.float32)
    if cuts:
        values = values * steps_of(own_key, extent, cuts, -0.22, 0.18)
    return jnp.clip(values, -limit, limit).astype(held_as)


def setup_inputs(seed: int = 0) -> dict:
    key_list = jax.random.split(jax.random.key(seed), 10)
    return {
        "schur_block": draw_schur_block(jax.random.fold_in(key_list[9], 71), 0),
        "load_cases": draw_load_cases(jax.random.fold_in(key_list[9], 71), 0),
        "precond_scale": jnp.clip(jnp.exp(math.log(2.0) - 1.3862944 * jax.random.uniform(key_list[2], (NCL, SUBS, W), jnp.float32) ** steps_of(key_list[2], (NCL, SUBS, W), ((0, 16), (1, 32)), -0.2, 0.2)), 0.5, 2.0),
        "coarse_basis": noise(key_list[3], (NCL, SUBS, NZ, W), (W // 32) ** -0.5, 1.0, ((0, 16), (1, 32)), jnp.float32),
        "coarse_inverse": draw_coarse_inverse(jax.random.fold_in(key_list[9], 71), 0),
        "corner_weight": jnp.clip(jnp.exp(math.log(4.0) - 2.0794415 * jax.random.uniform(key_list[5], (NCL, KC), jnp.float32) ** steps_of(key_list[5], (NCL, KC), ((0, 16), (1, 32)), -0.2, 0.2)), 0.5, 4.0),
        "corner_index": with_ends(jax.random.randint(key_list[6], (NCL, SUBS, NC), 0, KC), jax.random.fold_in(key_list[6], 1), 0, KC - 1).astype(jnp.int32),
        "iface_block": with_ends(jax.random.randint(key_list[7], (NCL, SUBS, 2), 0, NB), jax.random.fold_in(key_list[7], 1), 0, NB - 1).astype(jnp.int32),
        "glue_link": with_ends((jax.random.randint(key_list[8], (NCL, SUBS), 0, 4) < 3).astype(jnp.int32), jax.random.fold_in(key_list[8], 1), 0, 1),
    }


highest = lax.Precision.HIGHEST


def cut_block(vector, offset):
    return lax.dynamic_slice_in_dim(vector, offset, NI, 0)


def add_block(vector, addend, offset):
    return lax.dynamic_update_slice_in_dim(vector, lax.dynamic_slice_in_dim(vector, offset, NI, 0) + addend, offset, 0)


def apply_operator(field, schur_block, corner_weight, corner_index, iface_block, glue_link):
    rounded = field.astype(jnp.bfloat16).astype(jnp.float32)

    def one_cluster(inputs):
        blocks_here, vectors = inputs
        return jnp.einsum("swv,svr->swr", blocks_here.astype(jnp.float32), vectors, precision=highest)

    applied = lax.map(one_cluster, (schur_block, rounded))

    def corner_cluster(inputs):
        corner_rows, numbers, gains_here = inputs
        totals = jax.ops.segment_sum(corner_rows.reshape(-1, corner_rows.shape[-1]), numbers.reshape(-1), num_segments=KC)
        scaled = totals * gains_here[:, None]
        return scaled[numbers]

    back = lax.map(corner_cluster, (field[:, :, :NC, :], corner_index, corner_weight))
    applied = applied.at[:, :, :NC, :].add(back)
    left_row = (NC + iface_block[:, :, 0] * NI).astype(jnp.int32)
    right_row = (NC + iface_block[:, :, 1] * NI).astype(jnp.int32)
    cut_blocks = jax.vmap(jax.vmap(cut_block))
    add_blocks = jax.vmap(jax.vmap(add_block))
    left_block = cut_blocks(field, left_row)
    right_block = cut_blocks(field, right_row)
    glue_flag = glue_link.astype(jnp.float32)[:, :, None, None]
    next_left = jnp.roll(left_block, -1, axis=0)
    prev_right = jnp.roll(right_block, 1, axis=0)
    prev_glue = jnp.roll(glue_flag, 1, axis=0)
    jump_right = glue_flag * (right_block - next_left)
    jump_left = prev_glue * (prev_right - left_block)
    applied = add_blocks(applied, jump_right, right_row)
    applied = add_blocks(applied, -jump_left, left_row)
    return applied


def precondition(vector, precond_scale, coarse_basis, coarse_inverse):
    pieces = jnp.einsum("csnw,cswr->csnr", coarse_basis, vector, precision=highest)
    gathered = pieces.reshape(pieces.shape[0], -1, pieces.shape[-1])
    coarse = jnp.einsum("cij,cjr->cir", coarse_inverse, gathered, precision=highest).reshape(pieces.shape)
    return precond_scale[..., None] * vector + jnp.einsum("csnw,csnr->cswr", coarse_basis, coarse, precision=highest)


def inner(first_vec, second_vec):
    return jnp.sum(first_vec * second_vec, axis=(0, 1, 2))


def reference(schur_block, load_cases, precond_scale, coarse_basis, coarse_inverse, corner_weight, corner_index, iface_block, glue_link):
    solution = jnp.zeros_like(load_cases)
    residual = load_cases
    precond = precondition(residual, precond_scale, coarse_basis, coarse_inverse)
    direction = precond
    rho_now = inner(residual, precond)
    for iteration in range(ITERS):
        applied = apply_operator(direction, schur_block, corner_weight, corner_index, iface_block, glue_link)
        step_size = rho_now / inner(direction, applied)
        solution = solution + step_size * direction
        if iteration + 1 < ITERS:
            residual = residual - step_size * applied
            precond = precondition(residual, precond_scale, coarse_basis, coarse_inverse)
            rho_next = inner(residual, precond)
            direction = precond + (rho_next / rho_now) * direction
            rho_now = rho_next
    return solution
```

```python
import functools

import jax
import jax.numpy as jnp
from jax import lax
from jax.experimental import pallas as pl
from jax.experimental.pallas import tpu as pltpu
from jax.sharding import PartitionSpec as P

NC = 64
NI = 128
ITERS = 3
f32 = jnp.float32
bf16 = jnp.bfloat16


def dot(a, b, dims=((1,), (0,))):
    return lax.dot_general(
        a, b, (dims, ((), ())), precision=lax.Precision.HIGHEST, preferred_element_type=f32
    )


def iota(shape, dim):
    return lax.broadcasted_iota(jnp.int32, shape, dim)


def kernel(
    n_sub, n_cl,
    s_hbm, loads_ref, scale_ref, basis_ref, inv_ref, weight_ref, corner_ref, iface_ref, glue_ref,
    out_ref,
    smat, b8, bt, dmat, zv, dv, xv, sv, qv,
    ohT, oh, ct, invx, inv_own, e_scr, ccol, wcol,
    st_src, st_buf,
    p1_src, p1_buf, rs_src, rs_buf, ag_src, ag_buf, p2_src, p2_buf, gl_src, gl_buf,
    tq, td, tz,
    load_sem, st_sem, p1_sem, rs_sem, ag_sem, p2_sem, gl_sem,
):
    me = lax.axis_index("sub")
    cl = lax.axis_index("cluster")
    n_rows = loads_ref.shape[0]
    r_cols = loads_ref.shape[1]
    nz, cm = basis_ref.shape[0], inv_ref.shape[1]
    own = weight_ref.shape[1]
    half = own // 2
    nb = (n_rows - NC) // NI
    wst = st_src.shape[1]
    blk = 8 * n_sub

    load = pltpu.make_async_copy(s_hbm, smat, load_sem)
    load.start()

    barrier = pltpu.get_barrier_semaphore()

    @pl.loop(1, n_sub)
    def _(step):
        pl.semaphore_signal(barrier, inc=1, device_id={"sub": lax.rem(me + step, n_sub)})

    @pl.loop(1, n_cl)
    def _(step):
        pl.semaphore_signal(barrier, inc=1, device_id={"cluster": lax.rem(cl + step, n_cl)})

    def spread(src_of, buf, sem, axis, here, n):
        @pl.loop(1, n)
        def _(step):
            peer = lax.rem(here + step, n)
            pltpu.make_async_remote_copy(
                src_ref=src_of(peer),
                dst_ref=buf.at[here],
                send_sem=sem.at[0],
                recv_sem=sem.at[1],
                device_id={axis: peer},
            ).start()

    def drain(buf, sem, which, n):
        view = buf.at[pl.ds(0, n - 1)]
        pltpu.make_async_copy(view, view, sem.at[which]).wait()

    b8[0:nz, :] = basis_ref[...]
    b8[nz:nz + 1, :] = scale_ref[...]
    b8[nz + 1:8, :] = jnp.zeros((7 - nz, n_rows), f32)
    bt[...] = jnp.transpose(b8[...])
    pick = ((iota((8, r_cols), 0) == nz)).astype(f32)
    dmat[...] = dot(bt[...], pick)
    b8[nz:nz + 1, :] = jnp.zeros((1, n_rows), f32)

    corner_row = corner_ref[...]
    eye = iota((NC, NC), 0) == iota((NC, NC), 1)
    ccol[...] = jnp.sum(jnp.where(eye, corner_row, 0), axis=1, keepdims=True)

    m = iota((blk, NC), 0)
    base = (m >> 3) * own + (m & 7)
    oh[:, 0:NC] = (base == corner_row).astype(f32)
    oh[:, NC:2 * NC] = (base + half == corner_row).astype(f32)
    m = iota((NC, blk), 1)
    base = (m >> 3) * own + (m & 7)
    ohT[0:NC, :] = (base == ccol[...]).astype(f32)
    ohT[NC:2 * NC, :] = (base + half == ccol[...]).astype(f32)

    st_src[...] = jnp.zeros(st_src.shape, f32)
    st_src[0:nz, 0:cm] = inv_ref[...]
    st_src[0:nz, wst - NC:wst] = basis_ref[:, 0:NC]
    st_src[nz:nz + 1, wst - NC:wst] = corner_row.astype(f32)
    st_src[nz + 1:nz + 2, wst - NC:wst - NC + own] = weight_ref[...]

    ea, eb = iota((wst, blk), 0), iota((wst, blk), 1)
    expand = ((ea == (eb >> 3) * nz + (eb & 7)) & ((eb & 7) < nz) & (ea < cm)).astype(f32)
    row_ok = iota((8, wst), 0) < nz
    inv_own[...] = dot(jnp.where(row_ok, st_src[...], 0.0), expand)

    def packed_corners(v):
        z = jnp.zeros((NC, r_cols), f32)
        vv = jnp.concatenate(
            [jnp.concatenate([v, z], axis=1), jnp.concatenate([z, v], axis=1)], axis=0
        )
        return dot(oh[...], vv)

    def first_message(k, vec, sums):
        pieces = dot(b8[...], vec)
        zero = jnp.zeros((8 - len(sums), r_cols), f32)
        msg = jnp.concatenate([pieces, jnp.concatenate(list(sums) + [zero], axis=0)], axis=1)
        p1_src[k] = msg
        p1_buf[k, me] = msg

    def send_first(k):
        spread(lambda peer: p1_src.at[k], p1_buf.at[k], p1_sem.at[k], "sub", me, n_sub)

    def corner_message(k, vec):
        rs_src[k] = packed_corners(vec).reshape(n_sub, 8, 2 * r_cols)
        rs_buf[k, me] = rs_src[k, me]

    def send_corners(k):
        spread(lambda peer: rs_src.at[k, peer], rs_buf.at[k], rs_sem.at[k], "sub", me, n_sub)

    def own_corners(k):
        drain(rs_buf.at[k], rs_sem.at[k], 1, n_sub)
        total = jnp.sum(rs_buf[k], axis=0)
        ag_src[k] = total
        ag_buf[k, me] = total
        spread(lambda peer: ag_src.at[k], ag_buf.at[k], ag_sem.at[k], "sub", me, n_sub)

    def corner_back(k):
        drain(ag_buf.at[k], ag_sem.at[k], 1, n_sub)
        got = ag_buf[k].reshape(blk, 2 * r_cols)
        quad = dot(ohT[...], got)
        return quad[0:NC, 0:r_cols] + quad[NC:2 * NC, r_cols:2 * r_cols]

    glue_here = glue_ref[...].astype(f32)
    hi = NI // 2

    def placed(side, b):
        return (iface_ref[0:1, 1 - side:2 - side] == b).astype(f32)

    def block_of(side):
        rows = jnp.zeros((NI, r_cols), f32)
        for b in range(nb):
            rows = rows + placed(side, b) * dv[NC + b * NI:NC + (b + 1) * NI, :]
        return rows

    def send_glue(k):
        for side in range(2):
            rows = block_of(side)
            gl_src[k, side, 0:hi, :] = jnp.concatenate([rows[0:hi], rows[hi:NI]], axis=1)
            gl_src[k, side, hi:hi + 8, :] = jnp.broadcast_to(glue_here, (8, 2 * r_cols))
        for side, peer in ((0, lax.rem(cl + 1, n_cl)), (1, lax.rem(cl + n_cl - 1, n_cl))):
            pltpu.make_async_remote_copy(
                src_ref=gl_src.at[k, side],
                dst_ref=gl_buf.at[k, side],
                send_sem=gl_sem.at[k, side, 0],
                recv_sem=gl_sem.at[k, side, 1],
                device_id={"cluster": peer},
            ).start()

    def glue_wait(k, which):
        for side in range(2):
            pltpu.make_async_copy(
                gl_src.at[k, side], gl_buf.at[k, side], gl_sem.at[k, side, which]
            ).wait()

    def unpack(k, side):
        a = gl_buf[k, side, 0:hi, :]
        return jnp.concatenate([a[:, 0:r_cols], a[:, r_cols:2 * r_cols]], axis=0)

    loads = loads_ref[...]
    scaled = dmat[...] * loads
    first_message(0, loads, [jnp.sum(scaled * loads, axis=0, keepdims=True)])
    corner_message(0, scaled[0:NC, :])
    st_buf[me] = st_src[...]

    pl.semaphore_wait(barrier, n_sub + n_cl - 2)

    send_first(0)
    send_corners(0)
    spread(lambda peer: st_src, st_buf, st_sem, "sub", me, n_sub)

    drain(p1_buf.at[0], p1_sem.at[0], 1, n_sub)
    got = p1_buf[0].reshape(blk, 2 * r_cols)
    e_own = dot(inv_own[...], got)[:, 0:r_cols]
    zv[...] = dmat[...] * loads + dot(bt[...], e_own * (iota((8, r_cols), 0) < nz).astype(f32))
    dv[...] = zv[...]
    send_glue(0)
    own_corners(0)
    load.wait()

    def product():
        sv[...] = jnp.dot(smat[...], dv[...].astype(bf16), preferred_element_type=f32)

    product()

    drain(st_buf, st_sem, 1, n_sub)
    ws = jnp.zeros((NC, 1), f32)
    lane = iota((NC, NC), 1)
    row8 = iota((8, NC), 0) < nz
    for s in range(n_sub):
        tile = st_buf[s, :, wst - NC:wst]
        match = (ccol[...].astype(f32) == tile[nz:nz + 1, :]).astype(f32)
        ct[8 * s:8 * s + 8, :] = dot(jnp.where(row8, tile, 0.0), match, ((1,), (1,)))
        mine = (ccol[...] == s * own + lane) & (lane < own)
        ws = ws + jnp.sum(jnp.where(mine, tile[nz + 1:nz + 2, :], 0.0), axis=1, keepdims=True)
    wcol[...] = ws
    rows_ok = ((iota((blk, wst), 0) & 7) < nz) & (iota((blk, wst), 1) < cm)
    invx[...] = dot(jnp.where(rows_ok, st_buf[...].reshape(blk, wst), 0.0), expand)

    def coarse(k):
        got = p1_buf[k].reshape(blk, 2 * r_cols)
        e_all = dot(invx[...], got)
        e_scr[...] = e_all[:, 0:r_cols]
        quad = jnp.sum((got * e_all)[:, 0:r_cols], axis=0, keepdims=True)
        return quad, jnp.sum(p1_buf[k], axis=0)[:, r_cols:2 * r_cols]

    quad, sums = coarse(0)
    rho_part = sums[0:1, :] + quad
    tz[...] = corner_back(0) + dot(ct[...], e_scr[...], ((0,), (0,)))
    td[...] = tz[...]
    xv[...] = jnp.zeros_like(xv)

    def finish_product(k):
        sv[0:NC, :] = sv[0:NC, :] + wcol[...] * td[...]
        glue_wait(k, 1)
        next_left = unpack(k, 1)
        prev_right = unpack(k, 0)
        prev_glue = gl_buf[k, 0, hi:hi + 1, 0:r_cols]
        jump_right = glue_here * (block_of(0) - next_left)
        jump_left = prev_glue * (prev_right - block_of(1))
        for b in range(nb):
            rows = slice(NC + b * NI, NC + (b + 1) * NI)
            sv[rows, :] = sv[rows, :] + placed(0, b) * jump_right - placed(1, b) * jump_left

    rho = None
    for k in range(ITERS):
        last = k + 1 == ITERS
        finish_product(k)
        s, d = sv[...], dv[...]
        sums = [jnp.sum(d * s, axis=0, keepdims=True)]
        if not last:
            ds = dmat[...] * s
            sums.append(jnp.sum(zv[...] * s, axis=0, keepdims=True))
            sums.append(jnp.sum(ds * s, axis=0, keepdims=True))
            first_message(k + 1, s, sums)
            send_first(k + 1)
            corner_message(k + 1, ds[0:NC, :])
            send_corners(k + 1)
        else:
            first_message(k + 1, s, sums)
            send_first(k + 1)
        drain(p1_buf.at[k + 1], p1_sem.at[k + 1], 1, n_sub)
        if not last:
            quad, sums = coarse(k + 1)
            parts = [sums[0:1], sums[1:2], sums[2:3] + quad]
        else:
            sums = jnp.sum(p1_buf[k + 1], axis=0)[:, r_cols:2 * r_cols]
            parts = [sums[0:1], sums[1:2], sums[2:3]]
        msg = jnp.concatenate(
            [
                jnp.concatenate([parts[0], parts[1]], axis=1),
                jnp.concatenate([parts[2], rho_part], axis=1),
            ],
            axis=0,
        )
        p2_src[k] = msg
        p2_buf[k, cl] = msg
        spread(lambda peer: p2_src.at[k], p2_buf.at[k], p2_sem.at[k], "cluster", cl, n_cl)
        if not last:
            e_own = e_scr[pl.ds(8 * me, 8), :]
            q = ds + dot(bt[...], e_own)
            qv[...] = q
            tq[...] = dot(ct[...], e_scr[...], ((0,), (0,)))
            own_corners(k + 1)
        drain(p2_buf.at[k], p2_sem.at[k], 1, n_cl)
        total = jnp.sum(p2_buf[k], axis=0)
        curve = total[0:1, 0:r_cols]
        if k == 0:
            rho = total[1:2, r_cols:2 * r_cols]
        step = rho / curve
        if last:
            out_ref[...] = xv[...] + step * dv[...]
            break
        xv[...] = xv[...] + step * dv[...]
        zs = total[0:1, r_cols:2 * r_cols]
        sq = total[1:2, 0:r_cols]
        rho_next = rho - 2.0 * step * zs + step * (step * sq)
        beta = rho_next / rho
        z = zv[...] - step * qv[...]
        zv[...] = z
        dv[...] = z + beta * dv[...]
        rho = rho_next
        send_glue(k + 1)
        product()
        tz[...] = tz[...] - step * (tq[...] + corner_back(k + 1))
        td[...] = tz[...] + beta * td[...]

    drain(st_buf, st_sem, 0, n_sub)
    for k in range(ITERS + 1):
        drain(p1_buf.at[k], p1_sem.at[k], 0, n_sub)
    for k in range(ITERS):
        drain(rs_buf.at[k], rs_sem.at[k], 0, n_sub)
        drain(ag_buf.at[k], ag_sem.at[k], 0, n_sub)
        drain(p2_buf.at[k], p2_sem.at[k], 0, n_cl)
        glue_wait(k, 0)


def per_device(
    n_sub, n_cl, schur_block, load_cases, precond_scale, coarse_basis, coarse_inverse,
    corner_weight, corner_index, iface_block, glue_link,
):
    n_rows, r = load_cases.shape[2:]
    nz, cm = coarse_basis.shape[2], coarse_inverse.shape[2]
    blk = 8 * n_sub
    wst = -(-(cm + NC) // 128) * 128
    vec = pltpu.VMEM((n_rows, r), f32)
    vmem = pl.BlockSpec(memory_space=pltpu.VMEM)
    dma = pltpu.SemaphoreType.DMA
    out = pl.pallas_call(
        functools.partial(kernel, n_sub, n_cl),
        out_shape=jax.ShapeDtypeStruct((n_rows, r), f32),
        in_specs=[pl.BlockSpec(memory_space=pl.ANY)] + [vmem] * 8,
        out_specs=vmem,
        scratch_shapes=[
            pltpu.VMEM((n_rows, n_rows), bf16),
            pltpu.VMEM((8, n_rows), f32),
            pltpu.VMEM((n_rows, 8), f32),
            vec, vec, vec, vec, vec, vec,
            pltpu.VMEM((2 * NC, blk), f32),
            pltpu.VMEM((blk, 2 * NC), f32),
            pltpu.VMEM((blk, NC), f32),
            pltpu.VMEM((blk, blk), f32),
            pltpu.VMEM((8, blk), f32),
            pltpu.VMEM((blk, r), f32),
            pltpu.VMEM((NC, 1), jnp.int32),
            pltpu.VMEM((NC, 1), f32),
            pltpu.VMEM((8, wst), f32),
            pltpu.VMEM((n_sub, 8, wst), f32),
            pltpu.VMEM((ITERS + 1, 8, 2 * r), f32),
            pltpu.VMEM((ITERS + 1, n_sub, 8, 2 * r), f32),
            pltpu.VMEM((ITERS, n_sub, 8, 2 * r), f32),
            pltpu.VMEM((ITERS, n_sub, 8, 2 * r), f32),
            pltpu.VMEM((ITERS, 8, 2 * r), f32),
            pltpu.VMEM((ITERS, n_sub, 8, 2 * r), f32),
            pltpu.VMEM((ITERS, 2, 2 * r), f32),
            pltpu.VMEM((ITERS, n_cl, 2, 2 * r), f32),
            pltpu.VMEM((ITERS, 2, NI // 2 + 8, 2 * r), f32),
            pltpu.VMEM((ITERS, 2, NI // 2 + 8, 2 * r), f32),
            pltpu.VMEM((NC, r), f32),
            pltpu.VMEM((NC, r), f32),
            pltpu.VMEM((NC, r), f32),
            dma(()),
            dma((2,)),
            dma((ITERS + 1, 2)),
            dma((ITERS, 2)),
            dma((ITERS, 2)),
            dma((ITERS, 2)),
            dma((ITERS, 2, 2)),
        ],
        compiler_params=pltpu.CompilerParams(
            collective_id=0, has_side_effects=True, vmem_limit_bytes=48 * 1024 * 1024
        ),
    )(
        schur_block[0, 0], load_cases[0, 0], precond_scale[0], coarse_basis[0, 0],
        coarse_inverse[0], corner_weight, corner_index[0], iface_block[0], glue_link,
    )
    return out[None, None]


def solution(mesh):
    in_specs = (
        P("cluster", "sub", None, None),
        P("cluster", "sub", None, None),
        P("cluster", "sub", None),
        P("cluster", "sub", None, None),
        P("cluster", "sub", None),
        P("cluster", "sub"),
        P("cluster", "sub", None),
        P("cluster", "sub", None),
        P("cluster", "sub"),
    )
    return jax.shard_map(
        functools.partial(per_device, mesh.shape["sub"], mesh.shape["cluster"]),
        mesh=mesh, in_specs=in_specs, out_specs=P("cluster", "sub", None, None), check_vma=False,
    )
```

```python
import functools

import jax
import jax.numpy as jnp
from jax import lax
from jax.experimental import pallas as pl
from jax.experimental.pallas import tpu as pltpu
from jax.sharding import PartitionSpec as P

NC = 64
NI = 128
ITERS = 3
f32 = jnp.float32
bf16 = jnp.bfloat16


def dot(a, b, dims=((1,), (0,))):
    return lax.dot_general(
        a, b, (dims, ((), ())), precision=lax.Precision.HIGHEST, preferred_element_type=f32
    )


def iota(shape, dim):
    return lax.broadcasted_iota(jnp.int32, shape, dim)


def kernel(
    n_sub, n_cl,
    s_hbm, loads_hbm, scale_hbm, basis_hbm, inv_hbm, weight_hbm, corner_hbm, iface_hbm, glue_hbm,
    out_ref,
    smat, loads_t, scale_ref, basis_ref, inv_ref, weight_ref, corner_ref, iface_ref, glue_ref,
    lv, nld, prd, nlz, prz, scol,
    b8, bt, dmat, zv, dv, xv, sv, qv,
    ohT, oh, ct, invx, inv_own, e_scr, ccol, wcol,
    st_src, st_buf,
    p1_src, p1_buf, rs_src, rs_buf, ag_src, ag_buf, p2_src, p2_buf, gl_src, gl_buf,
    tq, td, tz,
    load_sem, st_sem, p1_sem, rs_sem, ag_sem, p2_sem, gl_sem,
):
    me = lax.axis_index("sub")
    cl = lax.axis_index("cluster")
    r_cols, n_rows = loads_t.shape
    nz, cm = basis_ref.shape[0], inv_ref.shape[2]
    own = weight_ref.shape[1]
    half = own // 2
    nb = (n_rows - NC) // NI
    wst = st_src.shape[1]
    blk = 8 * n_sub

    barrier = pltpu.get_barrier_semaphore()

    @pl.loop(1, n_sub)
    def _(step):
        pl.semaphore_signal(barrier, inc=1, device_id={"sub": lax.rem(me + step, n_sub)})

    @pl.loop(1, n_cl)
    def _(step):
        pl.semaphore_signal(barrier, inc=1, device_id={"cluster": lax.rem(cl + step, n_cl)})

    fields = (
        (loads_hbm, loads_t), (basis_hbm, basis_ref), (scale_hbm, scale_ref), (inv_hbm, inv_ref),
        (corner_hbm, corner_ref), (weight_hbm, weight_ref), (iface_hbm, iface_ref),
        (glue_hbm, glue_ref), (s_hbm, smat),
    )
    copies = [pltpu.make_async_copy(a, b, load_sem.at[i]) for i, (a, b) in enumerate(fields)]
    for copy in copies:
        copy.start()

    def spread(src_of, buf, sem, axis, here, n, rows=8):
        @pl.loop(0, n - 1)
        def _(i):
            sign = 1 - 2 * lax.rem(i, 2)
            peer = lax.rem(here + n // 2 + sign * lax.div(i + 1, 2), n)
            pltpu.make_async_remote_copy(
                src_ref=src_of(peer).at[pl.ds(0, rows)],
                dst_ref=buf.at[here, pl.ds(0, rows)],
                send_sem=sem.at[0],
                recv_sem=sem.at[1],
                device_id={axis: peer},
            ).start()

    def drain(buf, sem, which, n, rows=8):
        view = buf.at[pl.ds(0, n - 1), pl.ds(0, rows)]
        pltpu.make_async_copy(view, view, sem.at[which]).wait()

    for copy in copies[:-1]:
        copy.wait()
    for i in range(nz):
        b8[i:i + 1, :] = basis_ref[i]
    b8[nz:nz + 1, :] = scale_ref[...]
    b8[nz + 1:8, :] = jnp.zeros((7 - nz, n_rows), f32)
    bt[...] = jnp.transpose(b8[...])
    pick = ((iota((8, r_cols), 0) == nz)).astype(f32)
    dmat[...] = dot(bt[...], pick)
    b8[nz:nz + 1, :] = jnp.zeros((1, n_rows), f32)

    corner_row = corner_ref[...]
    eye = iota((NC, NC), 0) == iota((NC, NC), 1)
    ccol[...] = jnp.sum(jnp.where(eye, corner_row, 0), axis=1, keepdims=True)

    m = iota((blk, NC), 0)
    base = (m >> 3) * own + (m & 7)
    oh[:, 0:NC] = (base == corner_row).astype(f32)
    oh[:, NC:2 * NC] = (base + half == corner_row).astype(f32)
    m = iota((NC, blk), 1)
    base = (m >> 3) * own + (m & 7)
    ohT[0:NC, :] = (base == ccol[...]).astype(f32)
    ohT[NC:2 * NC, :] = (base + half == ccol[...]).astype(f32)

    st_src[...] = jnp.zeros(st_src.shape, f32)
    for i in range(nz):
        st_src[i:i + 1, 0:cm] = inv_ref[i]
    st_src[0:nz, wst - NC:wst] = b8[0:nz, 0:NC]
    st_src[nz:nz + 1, 0:NC] = scale_ref[:, 0:NC]
    st_src[nz:nz + 1, wst - NC:wst] = corner_row.astype(f32)
    st_src[nz + 1:nz + 2, wst - NC:wst - NC + own] = weight_ref[...]

    ea, eb = iota((wst, blk), 0), iota((wst, blk), 1)
    expand = ((ea == (eb >> 3) * nz + (eb & 7)) & ((eb & 7) < nz) & (ea < cm)).astype(f32)
    row_ok = iota((8, wst), 0) < nz
    inv_own[...] = dot(jnp.where(row_ok, st_src[...], 0.0), expand)

    def packed_corners(v):
        z = jnp.zeros((NC, r_cols), f32)
        vv = jnp.concatenate(
            [jnp.concatenate([v, z], axis=1), jnp.concatenate([z, v], axis=1)], axis=0
        )
        return dot(oh[...], vv)

    tail = jnp.zeros((3, r_cols), f32)

    def first_message(k, vec, sums):
        pieces = dot(b8[...], vec)
        sums = list(sums) + [jnp.zeros((1, r_cols), f32)] * (4 - len(sums))
        msg = jnp.concatenate(
            [
                jnp.concatenate([pieces[0:3], sums[0], sums[1], tail], axis=0),
                jnp.concatenate([pieces[3:6], sums[2], sums[3], tail], axis=0),
            ],
            axis=1,
        )
        p1_src[k] = msg
        p1_buf[k, me] = msg

    def send_first(k):
        spread(lambda peer: p1_src.at[k], p1_buf.at[k], p1_sem.at[k], "sub", me, n_sub, 5)

    def first_received(k):
        drain(p1_buf.at[k], p1_sem.at[k], 1, n_sub, 5)
        got = p1_buf[k]
        at = iota(got.shape, 1)
        got = jnp.where(at < 5, got, 0.0)
        moved = pltpu.roll(pltpu.roll(got, r_cols, 2), 3, 1)
        pieces = jnp.where(at < 3, got, jnp.where(at < nz, moved, 0.0))
        return pieces.reshape(blk, 2 * r_cols)[:, 0:r_cols], jnp.sum(got, axis=0)[3:5]

    def corner_message(k, vec):
        rs_src[k] = packed_corners(vec).reshape(n_sub, 8, 2 * r_cols)
        rs_buf[k, me] = rs_src[k, me]

    def send_corners(k):
        spread(lambda peer: rs_src.at[k, peer], rs_buf.at[k], rs_sem.at[k], "sub", me, n_sub)

    def own_corners(k):
        drain(rs_buf.at[k], rs_sem.at[k], 1, n_sub)
        total = jnp.sum(rs_buf[k], axis=0)
        ag_src[k] = total
        ag_buf[k, me] = total
        spread(lambda peer: ag_src.at[k], ag_buf.at[k], ag_sem.at[k], "sub", me, n_sub)

    def corner_back(k):
        drain(ag_buf.at[k], ag_sem.at[k], 1, n_sub)
        got = ag_buf[k].reshape(blk, 2 * r_cols)
        quad = dot(ohT[...], got)
        return quad[0:NC, 0:r_cols] + quad[NC:2 * NC, r_cols:2 * r_cols]

    glue_here = glue_ref[...].astype(f32)
    hi = NI // 2

    def placed(side, b):
        return (iface_ref[0:1, 1 - side:2 - side] == b).astype(f32)

    def block_of(side, ref):
        rows = jnp.zeros((NI, r_cols), f32)
        for b in range(nb):
            rows = rows + placed(side, b) * ref[NC + b * NI:NC + (b + 1) * NI, :]
        return rows

    def send_glue(k, ref):
        for side in range(2):
            rows = block_of(side, ref)
            gl_src[k, side, 0:hi, :] = jnp.concatenate([rows[0:hi], rows[hi:NI]], axis=1)
            gl_src[k, side, hi:hi + 8, :] = jnp.broadcast_to(glue_here, (8, 2 * r_cols))
        for side, peer in ((0, lax.rem(cl + 1, n_cl)), (1, lax.rem(cl + n_cl - 1, n_cl))):
            pltpu.make_async_remote_copy(
                src_ref=gl_src.at[k, side],
                dst_ref=gl_buf.at[k, side],
                send_sem=gl_sem.at[k, side, 0],
                recv_sem=gl_sem.at[k, side, 1],
                device_id={"cluster": peer},
            ).start()

    def glue_wait(k, which):
        for side in range(2):
            pltpu.make_async_copy(
                gl_src.at[k, side], gl_buf.at[k, side], gl_sem.at[k, side, which]
            ).wait()

    def unpack(k, side):
        a = gl_buf[k, side, 0:hi, :]
        return jnp.concatenate([a[:, 0:r_cols], a[:, r_cols:2 * r_cols]], axis=0)

    lv[...] = jnp.transpose(loads_t[...])
    loads = lv[...]
    scaled = dmat[...] * loads
    corner_message(0, scaled[0:NC, :])
    first_message(0, loads, [jnp.sum(scaled * loads, axis=0, keepdims=True)])
    st_buf[me] = st_src[...]

    pl.semaphore_wait(barrier, n_sub + n_cl - 2)

    send_corners(0)
    send_first(0)
    spread(lambda peer: st_src, st_buf, st_sem, "sub", me, n_sub)
    copies[-1].wait()
    own_corners(0)
    first_pieces, first_sums = first_received(0)
    e_own = dot(inv_own[...], first_pieces)
    z = dmat[...] * lv[...] + dot(bt[...], e_own * (iota((8, r_cols), 0) < nz).astype(f32))
    zv[...] = z
    dv[...] = z

    def product(k, last):
        half_d = dv[...].astype(bf16)
        top = jnp.dot(smat[0:NC, :], half_d, preferred_element_type=f32)
        sv[0:NC, :] = top
        if not last:
            corner_message(k + 1, dmat[0:NC, :] * top)
            send_corners(k + 1)
        if k == 0:
            send_glue(0, zv)
        sv[NC:, :] = jnp.dot(smat[NC:, :], half_d, preferred_element_type=f32)

    product(0, False)

    drain(st_buf, st_sem, 1, n_sub)
    ws = jnp.zeros((NC, 1), f32)
    sc = jnp.zeros((NC, 1), f32)
    lane = iota((NC, NC), 1)
    row8 = iota((8, NC), 0) < nz
    for s in range(n_sub):
        tile = st_buf[s, :, wst - NC:wst]
        match = (ccol[...].astype(f32) == tile[nz:nz + 1, :]).astype(f32)
        ct[8 * s:8 * s + 8, :] = dot(jnp.where(row8, tile, 0.0), match, ((1,), (1,)))
        sc = sc + jnp.sum(match * st_buf[s, nz:nz + 1, 0:NC], axis=1, keepdims=True)
        mine = (ccol[...] == s * own + lane) & (lane < own)
        ws = ws + jnp.sum(jnp.where(mine, tile[nz + 1:nz + 2, :], 0.0), axis=1, keepdims=True)
    wcol[...] = ws
    scol[...] = sc * ws
    rows_ok = ((iota((blk, wst), 0) & 7) < nz) & (iota((blk, wst), 1) < cm)
    invx[...] = dot(jnp.where(rows_ok, st_buf[...].reshape(blk, wst), 0.0), expand)

    def coarse(pieces):
        e_all = dot(invx[...], pieces)
        e_scr[...] = e_all
        return jnp.sum(pieces * e_all, axis=0, keepdims=True)

    rho_part = first_sums[0:1, 0:r_cols] + coarse(first_pieces)
    tz[...] = corner_back(0) + dot(ct[...], e_scr[...], ((0,), (0,)))
    td[...] = tz[...]
    xv[...] = jnp.zeros_like(xv)

    def finish_product(k, step, beta):
        sv[0:NC, :] = sv[0:NC, :] + wcol[...] * td[...]
        glue_wait(k, 1)
        if k == 0:
            nlz[...] = unpack(k, 1)
            prz[...] = unpack(k, 0)
            nld[...] = nlz[...]
            prd[...] = prz[...]
        else:
            nlz[...] = nlz[...] - step * unpack(k, 1)
            prz[...] = prz[...] - step * unpack(k, 0)
            nld[...] = nlz[...] + beta * nld[...]
            prd[...] = prz[...] + beta * prd[...]
        prev_glue = gl_buf[0, 0, hi:hi + 1, 0:r_cols]
        jump_right = glue_here * (block_of(0, dv) - nld[...])
        jump_left = prev_glue * (prd[...] - block_of(1, dv))
        for b in range(nb):
            rows = slice(NC + b * NI, NC + (b + 1) * NI)
            sv[rows, :] = sv[rows, :] + placed(0, b) * jump_right - placed(1, b) * jump_left

    rho = step = beta = None
    for k in range(ITERS):
        last = k + 1 == ITERS
        finish_product(k, step, beta)
        s, d = sv[...], dv[...]
        curve_part = jnp.sum(d * s, axis=0, keepdims=True)
        if not last:
            ds = dmat[...] * s
            sums = [
                curve_part,
                jnp.sum(zv[...] * s, axis=0, keepdims=True),
                jnp.sum(ds * s, axis=0, keepdims=True),
            ]
            first_message(k + 1, s, sums)
            send_first(k + 1)
            own_corners(k + 1)
            pieces, sums = first_received(k + 1)
            quad = coarse(pieces)
            parts = [sums[0:1, 0:r_cols], sums[1:2, 0:r_cols], sums[0:1, r_cols:] + quad]
        else:
            msg = jnp.concatenate([curve_part, curve_part], axis=1)
            p1_src[k + 1, 0:1] = msg
            p1_buf[k + 1, me, 0:1] = msg
            spread(lambda peer: p1_src.at[k + 1], p1_buf.at[k + 1], p1_sem.at[k + 1],
                   "sub", me, n_sub, 1)
            drain(p1_buf.at[k + 1], p1_sem.at[k + 1], 1, n_sub, 1)
            sums = jnp.sum(p1_buf[k + 1, :, 0:1], axis=0)[:, 0:r_cols]
            parts = [sums, sums, sums]
        msg = jnp.concatenate(
            [
                jnp.concatenate([parts[0], parts[1]], axis=1),
                jnp.concatenate([parts[2], rho_part], axis=1),
            ],
            axis=0,
        )
        p2_src[k] = msg
        p2_buf[k, cl] = msg
        spread(lambda peer: p2_src.at[k], p2_buf.at[k], p2_sem.at[k], "cluster", cl, n_cl, 2)
        if not last:
            e_own = e_scr[pl.ds(8 * me, 8), :]
            qv[...] = ds + dot(bt[...], e_own)
            send_glue(k + 1, qv)
            tq[...] = scol[...] * td[...] + dot(ct[...], e_scr[...], ((0,), (0,)))
        drain(p2_buf.at[k], p2_sem.at[k], 1, n_cl, 2)
        total = jnp.sum(p2_buf[k], axis=0)
        curve = total[0:1, 0:r_cols]
        if k == 0:
            rho = total[1:2, r_cols:2 * r_cols]
        step = rho / curve
        if last:
            out_ref[...] = xv[...] + step * dv[...]
            break
        zs = total[0:1, r_cols:2 * r_cols]
        sq = total[1:2, 0:r_cols]
        rho_next = rho - 2.0 * step * zs + step * (step * sq)
        beta = rho_next / rho
        d = dv[...]
        z = zv[...] - step * qv[...]
        zv[...] = z
        dv[...] = z + beta * d
        xv[...] = xv[...] + step * d
        rho = rho_next
        product(k + 1, k + 2 == ITERS)
        tz[...] = tz[...] - step * (tq[...] + corner_back(k + 1))
        td[...] = tz[...] + beta * td[...]

    drain(st_buf, st_sem, 0, n_sub)
    for k in range(ITERS + 1):
        drain(p1_buf.at[k], p1_sem.at[k], 0, n_sub, 5 if k < ITERS else 1)
    for k in range(ITERS):
        drain(rs_buf.at[k], rs_sem.at[k], 0, n_sub)
        drain(ag_buf.at[k], ag_sem.at[k], 0, n_sub)
        drain(p2_buf.at[k], p2_sem.at[k], 0, n_cl, 2)
        glue_wait(k, 0)


def per_device(
    n_sub, n_cl, schur_block, load_cases, precond_scale, coarse_basis, coarse_inverse,
    corner_weight, corner_index, iface_block, glue_link,
):
    n_rows, r = load_cases.shape[2:]
    nz, cm = coarse_basis.shape[2], coarse_inverse.shape[2]
    blk = 8 * n_sub
    wst = -(-(cm + NC) // 128) * 128
    vec = pltpu.VMEM((n_rows, r), f32)
    vmem = pl.BlockSpec(memory_space=pltpu.VMEM)
    hbm = pl.BlockSpec(memory_space=pltpu.HBM)
    own = corner_weight.shape[1]
    dma = pltpu.SemaphoreType.DMA
    out = pl.pallas_call(
        functools.partial(kernel, n_sub, n_cl),
        out_shape=jax.ShapeDtypeStruct((n_rows, r), f32),
        in_specs=[hbm] * 9,
        out_specs=vmem,
        scratch_shapes=[
            pltpu.VMEM((n_rows, n_rows), bf16),
            pltpu.VMEM((r, n_rows), f32),
            pltpu.VMEM((1, n_rows), f32),
            pltpu.VMEM((nz, 1, n_rows), f32),
            pltpu.VMEM((nz, 1, cm), f32),
            pltpu.VMEM((1, own), f32),
            pltpu.VMEM((1, NC), jnp.int32),
            pltpu.VMEM((1, 2), jnp.int32),
            pltpu.VMEM((1, 1), jnp.int32),
            vec,
            pltpu.VMEM((NI, r), f32),
            pltpu.VMEM((NI, r), f32),
            pltpu.VMEM((NI, r), f32),
            pltpu.VMEM((NI, r), f32),
            pltpu.VMEM((NC, 1), f32),
            pltpu.VMEM((8, n_rows), f32),
            pltpu.VMEM((n_rows, 8), f32),
            vec, vec, vec, vec, vec, vec,
            pltpu.VMEM((2 * NC, blk), f32),
            pltpu.VMEM((blk, 2 * NC), f32),
            pltpu.VMEM((blk, NC), f32),
            pltpu.VMEM((blk, blk), f32),
            pltpu.VMEM((8, blk), f32),
            pltpu.VMEM((blk, r), f32),
            pltpu.VMEM((NC, 1), jnp.int32),
            pltpu.VMEM((NC, 1), f32),
            pltpu.VMEM((8, wst), f32),
            pltpu.VMEM((n_sub, 8, wst), f32),
            pltpu.VMEM((ITERS + 1, 8, 2 * r), f32),
            pltpu.VMEM((ITERS + 1, n_sub, 8, 2 * r), f32),
            pltpu.VMEM((ITERS, n_sub, 8, 2 * r), f32),
            pltpu.VMEM((ITERS, n_sub, 8, 2 * r), f32),
            pltpu.VMEM((ITERS, 8, 2 * r), f32),
            pltpu.VMEM((ITERS, n_sub, 8, 2 * r), f32),
            pltpu.VMEM((ITERS, 2, 2 * r), f32),
            pltpu.VMEM((ITERS, n_cl, 2, 2 * r), f32),
            pltpu.VMEM((ITERS, 2, NI // 2 + 8, 2 * r), f32),
            pltpu.VMEM((ITERS, 2, NI // 2 + 8, 2 * r), f32),
            pltpu.VMEM((NC, r), f32),
            pltpu.VMEM((NC, r), f32),
            pltpu.VMEM((NC, r), f32),
            dma((9,)),
            dma((2,)),
            dma((ITERS + 1, 2)),
            dma((ITERS, 2)),
            dma((ITERS, 2)),
            dma((ITERS, 2)),
            dma((ITERS, 2, 2)),
        ],
        compiler_params=pltpu.CompilerParams(
            collective_id=0, has_side_effects=True, vmem_limit_bytes=60 * 1024 * 1024
        ),
    )(
        schur_block[0, 0], load_cases[0, 0].T, precond_scale[0], jnp.swapaxes(coarse_basis[0], 0, 1),
        jnp.swapaxes(coarse_inverse, 0, 1), corner_weight, corner_index[0], iface_block[0], glue_link,
    )
    return out[None, None]


def solution(mesh):
    in_specs = (
        P("cluster", "sub", None, None),
        P("cluster", "sub", None, None),
        P("cluster", "sub", None),
        P("cluster", "sub", None, None),
        P("cluster", "sub", None),
        P("cluster", "sub"),
        P("cluster", "sub", None),
        P("cluster", "sub", None),
        P("cluster", "sub"),
    )
    return jax.shard_map(
        functools.partial(per_device, mesh.shape["sub"], mesh.shape["cluster"]),
        mesh=mesh, in_specs=in_specs, out_specs=P("cluster", "sub", None, None), check_vma=False,
    )
```

```python
import functools

import jax
import jax.numpy as jnp
from jax import lax
from jax.experimental import pallas as pl
from jax.experimental.pallas import tpu as pltpu
from jax.sharding import PartitionSpec as P

NC = 64
NI = 128
ITERS = 3
f32 = jnp.float32
bf16 = jnp.bfloat16


def mm(a, b, dims=((1,), (0,))):
    return lax.dot_general(a, b, (dims, ((), ())), preferred_element_type=f32)


def split(x):
    high = x.astype(bf16)
    return high, (x - high.astype(f32)).astype(bf16)


def split_rows(x):
    high, low = split(x)
    return jnp.concatenate([high.astype(f32), low.astype(f32)], axis=0).astype(bf16)


def halves_dot(pair, x):
    n = pair.shape[0] // 2
    high, low = split(x)
    both = mm(pair, high)
    return both[0:n] + both[n:2 * n] + mm(pair[0:n], low)


def iota(shape, dim):
    return lax.broadcasted_iota(jnp.int32, shape, dim)


def kernel(
    n_sub, n_cl,
    s_hbm, loads_hbm, scale_hbm, basis_hbm, inv_hbm, weight_hbm, corner_hbm, iface_hbm, glue_hbm,
    out_ref,
    smat, loads_t, scale_ref, basis_ref, inv_ref, weight_ref, corner_ref, iface_ref, glue_ref,
    lv, nld, prd, nlz, prz, scol,
    b8, bt, dmat, zv, dv, xv, sv, qv,
    ohT, oh, ct, ctt, invx, inv_own, grow, e_scr, ccol, wcol,
    st_src, st_buf,
    p1_src, p1_buf, rs_src, rs_buf, ag_src, ag_buf, p2_src, p2_buf, gl_src, gl_buf,
    tq, td, tz,
    load_sem, st_sem, p1_sem, rs_sem, ag_sem, p2_sem, gl_sem,
):
    me = lax.axis_index("sub")
    cl = lax.axis_index("cluster")
    r_cols, n_rows = loads_t.shape
    nz, cm = basis_ref.shape[0], inv_ref.shape[2]
    own = weight_ref.shape[1]
    half = own // 2
    nb = (n_rows - NC) // NI
    wst = st_src.shape[1]
    blk = 8 * n_sub

    barrier = pltpu.get_barrier_semaphore()

    @pl.loop(1, n_sub)
    def _(step):
        pl.semaphore_signal(barrier, inc=1, device_id={"sub": lax.rem(me + step, n_sub)})

    @pl.loop(1, n_cl)
    def _(step):
        pl.semaphore_signal(barrier, inc=1, device_id={"cluster": lax.rem(cl + step, n_cl)})

    fields = (
        (loads_hbm, loads_t), (basis_hbm, basis_ref), (scale_hbm, scale_ref), (inv_hbm, inv_ref),
        (corner_hbm, corner_ref), (weight_hbm, weight_ref), (iface_hbm, iface_ref),
        (glue_hbm, glue_ref), (s_hbm, smat),
    )
    copies = [pltpu.make_async_copy(a, b, load_sem.at[i]) for i, (a, b) in enumerate(fields)]
    for copy in copies:
        copy.start()

    def spread(src_of, buf, sem, axis, here, n, rows=8):
        @pl.loop(0, n - 1)
        def _(i):
            sign = 1 - 2 * lax.rem(i, 2)
            peer = lax.rem(here + n // 2 + sign * lax.div(i + 1, 2), n)
            pltpu.make_async_remote_copy(
                src_ref=src_of(peer).at[pl.ds(0, rows)],
                dst_ref=buf.at[here, pl.ds(0, rows)],
                send_sem=sem.at[0],
                recv_sem=sem.at[1],
                device_id={axis: peer},
            ).start()

    def drain(buf, sem, which, n, rows=8):
        view = buf.at[pl.ds(0, n - 1), pl.ds(0, rows)]
        pltpu.make_async_copy(view, view, sem.at[which]).wait()

    for copy in copies[:-1]:
        copy.wait()
    basis8 = jnp.concatenate([basis_ref[i] for i in range(nz)] + [jnp.zeros((8 - nz, n_rows), f32)], axis=0)
    b8[...] = split_rows(basis8)
    high, low = split(basis8)
    high, low = high.astype(f32), low.astype(f32)
    cols = jnp.transpose(
        jnp.concatenate([high, high, low, jnp.broadcast_to(scale_ref[...], (8, n_rows))], axis=0)
    )
    bt[...] = cols.astype(bf16)
    dmat[...] = jnp.broadcast_to(cols[:, 24:25], (n_rows, r_cols))

    corner_row = corner_ref[...]
    eye = iota((NC, NC), 0) == iota((NC, NC), 1)
    ccol[...] = jnp.sum(jnp.where(eye, corner_row, 0), axis=1, keepdims=True).astype(f32)
    corner_col = ccol[...].astype(jnp.int32)

    m = iota((blk, NC), 0)
    base = (m >> 3) * own + (m & 7)
    first, second = (base == corner_row).astype(f32), (base + half == corner_row).astype(f32)
    oh[...] = jnp.concatenate([first, second, first, second], axis=1).astype(bf16)
    m = iota((NC, blk), 1)
    base = (m >> 3) * own + (m & 7)
    pick = jnp.concatenate([base == corner_col, base + half == corner_col], axis=0)
    pick = pick.astype(f32).astype(bf16)
    ohT[...] = jnp.concatenate([pick, pick], axis=1)

    st_src[...] = jnp.zeros(st_src.shape, f32)
    for i in range(nz):
        st_src[i:i + 1, 0:cm] = inv_ref[i]
    st_src[0:nz, wst - NC:wst] = basis8[0:nz, 0:NC]
    st_src[nz:nz + 1, wst - NC:wst] = scale_ref[:, 0:NC]
    st_src[nz + 1:nz + 2, wst - NC:wst] = corner_row.astype(f32)
    st_src[nz + 1:nz + 2, 0:own] = weight_ref[...]

    ea, eb = iota((wst, blk), 0), iota((wst, blk), 1)
    grow[...] = (
        ((ea == (eb >> 3) * nz + (eb & 7)) & ((eb & 7) < nz) & (ea < cm)).astype(f32).astype(bf16)
    )
    row_ok = iota((8, wst), 0) < nz
    inv_own[...] = mm(split_rows(jnp.where(row_ok, st_src[...], 0.0)), grow[...]).astype(bf16)

    def packed_corners(v):
        zero = jnp.zeros((NC, r_cols), f32)
        parts = []
        for x in split(v):
            x = x.astype(f32)
            parts += [jnp.concatenate([x, zero], axis=1), jnp.concatenate([zero, x], axis=1)]
        return mm(oh[...], jnp.concatenate(parts, axis=0).astype(bf16))

    def basis_t(e):
        high, low = split(e)
        high, low = high.astype(f32), low.astype(f32)
        stack = jnp.concatenate([high, low, high, jnp.zeros((8, r_cols), f32)], axis=0)
        return mm(bt[...], stack.astype(bf16))

    tail = jnp.zeros((3, r_cols), f32)

    def first_message(k, vec, sums):
        pieces = halves_dot(b8[...], vec)
        sums = list(sums) + [jnp.zeros((1, r_cols), f32)] * (4 - len(sums))
        msg = jnp.concatenate(
            [
                jnp.concatenate([pieces[0:3], sums[0], sums[1], tail], axis=0),
                jnp.concatenate([pieces[3:6], sums[2], sums[3], tail], axis=0),
            ],
            axis=1,
        )
        p1_src[k] = msg
        p1_buf[k, me] = msg

    def send_first(k):
        spread(lambda peer: p1_src.at[k], p1_buf.at[k], p1_sem.at[k], "sub", me, n_sub, 5)

    def first_received(k):
        drain(p1_buf.at[k], p1_sem.at[k], 1, n_sub, 5)
        got = p1_buf[k]
        at = iota(got.shape, 1)
        got = jnp.where(at < 5, got, 0.0)
        moved = pltpu.roll(pltpu.roll(got, r_cols, 2), 3, 1)
        pieces = jnp.where(at < 3, got, jnp.where(at < nz, moved, 0.0))
        return pieces.reshape(blk, 2 * r_cols)[:, 0:r_cols], jnp.sum(got, axis=0)[3:5]

    def corner_message(k, vec):
        rs_src[k] = packed_corners(vec).reshape(n_sub, 8, 2 * r_cols)
        rs_buf[k, me] = rs_src[k, me]

    def send_corners(k):
        spread(lambda peer: rs_src.at[k, peer], rs_buf.at[k], rs_sem.at[k], "sub", me, n_sub)

    def own_corners(k):
        drain(rs_buf.at[k], rs_sem.at[k], 1, n_sub)
        total = jnp.sum(rs_buf[k], axis=0)
        ag_src[k] = total
        ag_buf[k, me] = total
        spread(lambda peer: ag_src.at[k], ag_buf.at[k], ag_sem.at[k], "sub", me, n_sub)

    def corner_back(k):
        drain(ag_buf.at[k], ag_sem.at[k], 1, n_sub)
        got = ag_buf[k].reshape(blk, 2 * r_cols)
        high, low = split(got)
        quad = mm(ohT[...], jnp.concatenate([high, low], axis=0))
        return quad[0:NC, 0:r_cols] + quad[NC:2 * NC, r_cols:2 * r_cols]

    glue_here = glue_ref[...].astype(f32)
    hi = NI // 2

    def placed(side, b):
        return (iface_ref[0:1, 1 - side:2 - side] == b).astype(f32)

    def block_of(side, ref):
        rows = jnp.zeros((NI, r_cols), f32)
        for b in range(nb):
            rows = rows + placed(side, b) * ref[NC + b * NI:NC + (b + 1) * NI, :]
        return rows

    def send_glue(k, ref):
        for side in range(2):
            rows = block_of(side, ref)
            gl_src[k, side, 0:hi, :] = jnp.concatenate([rows[0:hi], rows[hi:NI]], axis=1)
            gl_src[k, side, hi:hi + 8, :] = jnp.broadcast_to(glue_here, (8, 2 * r_cols))
        for side, peer in ((0, lax.rem(cl + 1, n_cl)), (1, lax.rem(cl + n_cl - 1, n_cl))):
            pltpu.make_async_remote_copy(
                src_ref=gl_src.at[k, side],
                dst_ref=gl_buf.at[k, side],
                send_sem=gl_sem.at[k, side, 0],
                recv_sem=gl_sem.at[k, side, 1],
                device_id={"cluster": peer},
            ).start()

    def glue_wait(k, which):
        for side in range(2):
            pltpu.make_async_copy(
                gl_src.at[k, side], gl_buf.at[k, side], gl_sem.at[k, side, which]
            ).wait()

    def unpack(k, side):
        a = gl_buf[k, side, 0:hi, :]
        return jnp.concatenate([a[:, 0:r_cols], a[:, r_cols:2 * r_cols]], axis=0)

    def spread_static():
        @pl.loop(1, n_sub // 2)
        def _(i):
            pltpu.make_async_remote_copy(
                src_ref=st_src,
                dst_ref=st_buf.at[core, place],
                send_sem=st_sem.at[0],
                recv_sem=st_sem.at[1],
                device_id={"sub": lax.rem(me + 2 * i, n_sub)},
            ).start()

    def pair_static():
        view = st_buf.at[0, pl.ds(0, n_sub // 2 - 1)]
        pltpu.make_async_copy(view, view, st_sem.at[1]).wait()
        pltpu.make_async_remote_copy(
            src_ref=st_buf.at[core],
            dst_ref=st_buf.at[core],
            send_sem=st_sem.at[2],
            recv_sem=st_sem.at[3],
            device_id={"sub": me + 1 - 2 * core},
        ).start()

    lv[...] = jnp.transpose(loads_t[...])
    loads = lv[...]
    scaled = dmat[...] * loads
    corner_message(0, scaled[0:NC, :])
    first_message(0, loads, [jnp.sum(scaled * loads, axis=0, keepdims=True)])
    core, place = lax.rem(me, 2), lax.div(me, 2)
    st_buf[core, place] = st_src[...]

    pl.semaphore_wait(barrier, n_sub + n_cl - 2)

    send_corners(0)
    send_first(0)
    spread_static()
    copies[-1].wait()
    own_corners(0)
    first_pieces, first_sums = first_received(0)
    z = dmat[...] * lv[...] + basis_t(halves_dot(inv_own[...], first_pieces))
    zv[...] = z
    dv[...] = z

    def product(k, last):
        half_d = dv[...].astype(bf16)
        top = jnp.dot(smat[0:NC, :], half_d, preferred_element_type=f32)
        sv[0:NC, :] = top
        if not last:
            corner_message(k + 1, dmat[0:NC, :] * top)
            send_corners(k + 1)
        if k == 0:
            send_glue(0, zv)
        sv[NC:, :] = jnp.dot(smat[NC:, :], half_d, preferred_element_type=f32)

    product(0, False)

    pair_static()
    pltpu.make_async_copy(st_buf.at[0], st_buf.at[0], st_sem.at[3]).wait()
    ws = jnp.zeros((NC, NC), f32)
    srow = jnp.zeros((1, NC), f32)
    lane = iota((NC, NC), 1).astype(f32)
    for s in range(n_sub):
        slot = st_buf[s % 2, s // 2]
        tile = slot[:, wst - NC:wst]
        match = (ccol[...] == tile[nz + 1:nz + 2, :]).astype(f32).astype(bf16)
        both = mm(split_rows(tile), match, ((1,), (1,)))
        rows = both[0:8] + both[8:16]
        ct[8 * s:8 * s + 8, :] = rows
        srow = srow + rows[nz:nz + 1, :]
        mine = (ccol[...] - float(s) * own == lane) & (lane < own)
        ws = ws + jnp.where(mine, slot[nz + 1:nz + 2, 0:NC], 0.0)
    wcol[...] = jnp.sum(ws, axis=1, keepdims=True)
    scol[...] = jnp.sum(jnp.where(eye, srow, 0.0), axis=1, keepdims=True) * wcol[...]
    ctt[...] = split_rows(jnp.transpose(ct[...]))
    row_ok = (iota((8, wst), 0) < nz) & (iota((8, wst), 1) < cm)
    stacked = jnp.concatenate(
        [jnp.where(row_ok, st_buf[s % 2, s // 2], 0.0) for s in range(n_sub)], axis=0
    )
    invx[...] = mm(split_rows(stacked), grow[...]).astype(bf16)

    def coarse(pieces):
        e_all = halves_dot(invx[...], pieces)
        e_scr[...] = e_all
        return jnp.sum(pieces * e_all, axis=0, keepdims=True)

    rho_part = first_sums[0:1, 0:r_cols] + coarse(first_pieces)
    tz[...] = corner_back(0) + halves_dot(ctt[...], e_scr[...])
    td[...] = tz[...]
    xv[...] = jnp.zeros_like(xv)

    def finish_product(k, step, beta):
        sv[0:NC, :] = sv[0:NC, :] + wcol[...] * td[...]
        glue_wait(k, 1)
        if k == 0:
            nlz[...] = unpack(k, 1)
            prz[...] = unpack(k, 0)
            nld[...] = nlz[...]
            prd[...] = prz[...]
        else:
            nlz[...] = nlz[...] - step * unpack(k, 1)
            prz[...] = prz[...] - step * unpack(k, 0)
            nld[...] = nlz[...] + beta * nld[...]
            prd[...] = prz[...] + beta * prd[...]
        prev_glue = gl_buf[0, 0, hi:hi + 1, 0:r_cols]
        jump_right = glue_here * (block_of(0, dv) - nld[...])
        jump_left = prev_glue * (prd[...] - block_of(1, dv))
        for b in range(nb):
            rows = slice(NC + b * NI, NC + (b + 1) * NI)
            sv[rows, :] = sv[rows, :] + placed(0, b) * jump_right - placed(1, b) * jump_left

    rho = step = beta = None
    for k in range(ITERS):
        last = k + 1 == ITERS
        finish_product(k, step, beta)
        s, d = sv[...], dv[...]
        curve_part = jnp.sum(d * s, axis=0, keepdims=True)
        if not last:
            ds = dmat[...] * s
            sums = [
                curve_part,
                jnp.sum(zv[...] * s, axis=0, keepdims=True),
                jnp.sum(ds * s, axis=0, keepdims=True),
            ]
            first_message(k + 1, s, sums)
            send_first(k + 1)
            own_corners(k + 1)
            pieces, sums = first_received(k + 1)
            quad = coarse(pieces)
            parts = [sums[0:1, 0:r_cols], sums[1:2, 0:r_cols], sums[0:1, r_cols:] + quad]
        else:
            msg = jnp.concatenate([curve_part, curve_part], axis=1)
            p1_src[k + 1, 0:1] = msg
            p1_buf[k + 1, me, 0:1] = msg
            spread(lambda peer: p1_src.at[k + 1], p1_buf.at[k + 1], p1_sem.at[k + 1],
                   "sub", me, n_sub, 1)
            drain(p1_buf.at[k + 1], p1_sem.at[k + 1], 1, n_sub, 1)
            sums = jnp.sum(p1_buf[k + 1, :, 0:1], axis=0)[:, 0:r_cols]
            parts = [sums, sums, sums]
        msg = jnp.concatenate(
            [
                jnp.concatenate([parts[0], parts[1]], axis=1),
                jnp.concatenate([parts[2], rho_part], axis=1),
            ],
            axis=0,
        )
        p2_src[k] = msg
        p2_buf[k, cl] = msg
        spread(lambda peer: p2_src.at[k], p2_buf.at[k], p2_sem.at[k], "cluster", cl, n_cl, 2)
        if not last:
            e_own = e_scr[pl.ds(8 * me, 8), :]
            qv[...] = ds + basis_t(e_own)
            send_glue(k + 1, qv)
            tq[...] = scol[...] * td[...] + halves_dot(ctt[...], e_scr[...])
        drain(p2_buf.at[k], p2_sem.at[k], 1, n_cl, 2)
        total = jnp.sum(p2_buf[k], axis=0)
        curve = total[0:1, 0:r_cols]
        if k == 0:
            rho = total[1:2, r_cols:2 * r_cols]
        step = rho / curve
        if last:
            out_ref[...] = xv[...] + step * dv[...]
            break
        zs = total[0:1, r_cols:2 * r_cols]
        sq = total[1:2, 0:r_cols]
        rho_next = rho - 2.0 * step * zs + step * (step * sq)
        beta = rho_next / rho
        d = dv[...]
        z = zv[...] - step * qv[...]
        zv[...] = z
        dv[...] = z + beta * d
        xv[...] = xv[...] + step * d
        rho = rho_next
        product(k + 1, k + 2 == ITERS)
        tz[...] = tz[...] - step * (tq[...] + corner_back(k + 1))
        td[...] = tz[...] + beta * td[...]

    view = st_buf.at[0, pl.ds(0, n_sub // 2 - 1)]
    pltpu.make_async_copy(view, view, st_sem.at[0]).wait()
    pltpu.make_async_copy(st_buf.at[0], st_buf.at[0], st_sem.at[2]).wait()
    for k in range(ITERS + 1):
        drain(p1_buf.at[k], p1_sem.at[k], 0, n_sub, 5 if k < ITERS else 1)
    for k in range(ITERS):
        drain(rs_buf.at[k], rs_sem.at[k], 0, n_sub)
        drain(ag_buf.at[k], ag_sem.at[k], 0, n_sub)
        drain(p2_buf.at[k], p2_sem.at[k], 0, n_cl, 2)
        glue_wait(k, 0)


def per_device(
    n_sub, n_cl, schur_block, load_cases, precond_scale, coarse_basis, coarse_inverse,
    corner_weight, corner_index, iface_block, glue_link,
):
    n_rows, r = load_cases.shape[2:]
    nz, cm = coarse_basis.shape[2], coarse_inverse.shape[2]
    blk = 8 * n_sub
    wst = -(-(cm + NC) // 128) * 128
    vec = pltpu.VMEM((n_rows, r), f32)
    vmem = pl.BlockSpec(memory_space=pltpu.VMEM)
    hbm = pl.BlockSpec(memory_space=pltpu.HBM)
    own = corner_weight.shape[1]
    dma = pltpu.SemaphoreType.DMA
    out = pl.pallas_call(
        functools.partial(kernel, n_sub, n_cl),
        out_shape=jax.ShapeDtypeStruct((n_rows, r), f32),
        in_specs=[hbm] * 9,
        out_specs=vmem,
        scratch_shapes=[
            pltpu.VMEM((n_rows, n_rows), bf16),
            pltpu.VMEM((r, n_rows), f32),
            pltpu.VMEM((1, n_rows), f32),
            pltpu.VMEM((nz, 1, n_rows), f32),
            pltpu.VMEM((nz, 1, cm), f32),
            pltpu.VMEM((1, own), f32),
            pltpu.VMEM((1, NC), jnp.int32),
            pltpu.VMEM((1, 2), jnp.int32),
            pltpu.VMEM((1, 1), jnp.int32),
            vec,
            pltpu.VMEM((NI, r), f32),
            pltpu.VMEM((NI, r), f32),
            pltpu.VMEM((NI, r), f32),
            pltpu.VMEM((NI, r), f32),
            pltpu.VMEM((NC, 1), f32),
            pltpu.VMEM((16, n_rows), bf16),
            pltpu.VMEM((n_rows, 32), bf16),
            vec, vec, vec, vec, vec, vec,
            pltpu.VMEM((2 * NC, 2 * blk), bf16),
            pltpu.VMEM((blk, 4 * NC), bf16),
            pltpu.VMEM((blk, NC), f32),
            pltpu.VMEM((2 * NC, blk), bf16),
            pltpu.VMEM((2 * blk, blk), bf16),
            pltpu.VMEM((16, blk), bf16),
            pltpu.VMEM((wst, blk), bf16),
            pltpu.VMEM((blk, r), f32),
            pltpu.VMEM((NC, 1), f32),
            pltpu.VMEM((NC, 1), f32),
            pltpu.VMEM((8, wst), f32),
            pltpu.VMEM((2, n_sub // 2, 8, wst), f32),
            pltpu.VMEM((ITERS + 1, 8, 2 * r), f32),
            pltpu.VMEM((ITERS + 1, n_sub, 8, 2 * r), f32),
            pltpu.VMEM((ITERS, n_sub, 8, 2 * r), f32),
            pltpu.VMEM((ITERS, n_sub, 8, 2 * r), f32),
            pltpu.VMEM((ITERS, 8, 2 * r), f32),
            pltpu.VMEM((ITERS, n_sub, 8, 2 * r), f32),
            pltpu.VMEM((ITERS, 2, 2 * r), f32),
            pltpu.VMEM((ITERS, n_cl, 2, 2 * r), f32),
            pltpu.VMEM((ITERS, 2, NI // 2 + 8, 2 * r), f32),
            pltpu.VMEM((ITERS, 2, NI // 2 + 8, 2 * r), f32),
            pltpu.VMEM((NC, r), f32),
            pltpu.VMEM((NC, r), f32),
            pltpu.VMEM((NC, r), f32),
            dma((9,)),
            dma((4,)),
            dma((ITERS + 1, 2)),
            dma((ITERS, 2)),
            dma((ITERS, 2)),
            dma((ITERS, 2)),
            dma((ITERS, 2, 2)),
        ],
        compiler_params=pltpu.CompilerParams(
            collective_id=0, has_side_effects=True, vmem_limit_bytes=40 * 1024 * 1024
        ),
    )(
        schur_block[0, 0], load_cases[0, 0].T, precond_scale[0], jnp.swapaxes(coarse_basis[0], 0, 1),
        jnp.swapaxes(coarse_inverse, 0, 1), corner_weight, corner_index[0], iface_block[0], glue_link,
    )
    return out[None, None]


def solution(mesh):
    in_specs = (
        P("cluster", "sub", None, None),
        P("cluster", "sub", None, None),
        P("cluster", "sub", None),
        P("cluster", "sub", None, None),
        P("cluster", "sub", None),
        P("cluster", "sub"),
        P("cluster", "sub", None),
        P("cluster", "sub", None),
        P("cluster", "sub"),
    )
    return jax.shard_map(
        functools.partial(per_device, mesh.shape["sub"], mesh.shape["cluster"]),
        mesh=mesh, in_specs=in_specs, out_specs=P("cluster", "sub", None, None), check_vma=False,
    )
```

```python
import functools

import jax
import jax.numpy as jnp
from jax import lax
from jax.experimental import pallas as pl
from jax.experimental.pallas import tpu as pltpu
from jax.sharding import PartitionSpec as P

NC = 64
NI = 128
ITERS = 3
f32 = jnp.float32
bf16 = jnp.bfloat16


def mm(a, b, dims=((1,), (0,))):
    return lax.dot_general(a, b, (dims, ((), ())), preferred_element_type=f32)


def split(x):
    high = x.astype(bf16)
    return high, (x - high.astype(f32)).astype(bf16)


def split_rows(x):
    high, low = split(x)
    return jnp.concatenate([high.astype(f32), low.astype(f32)], axis=0).astype(bf16)


def halves_dot(pair, x):
    n = pair.shape[0] // 2
    high, low = split(x)
    both = mm(pair, high)
    return both[0:n] + both[n:2 * n] + mm(pair[0:n], low)


def iota(shape, dim):
    return lax.broadcasted_iota(jnp.int32, shape, dim)


def kernel(
    n_sub, n_cl,
    s_hbm, loads_hbm, scale_hbm, basis_hbm, inv_hbm, weight_hbm, corner_hbm, iface_hbm, glue_hbm,
    out_ref,
    smat, loads_t, scale_ref, basis_ref, inv_ref, weight_ref, corner_ref, iface_ref, glue_ref,
    lv, nld, prd, nlz, prz, scol,
    b8, bt, dmat, zv, dv, xv, sv, qv,
    ohT, oh, ct, ctt, wide, invx, inv_own, grow, e_scr, ccol, wcol,
    st_src, st_buf,
    p1_src, p1_buf, rs_src, rs_buf, ag_src, ag_buf, p2_src, p2_buf, gl_src, gl_buf,
    tq, td, tz,
    load_sem, st_sem, p1_sem, rs_sem, ag_sem, p2_sem, gl_sem,
):
    me = lax.axis_index("sub")
    cl = lax.axis_index("cluster")
    r_cols, n_rows = loads_t.shape
    nz, cm = basis_ref.shape[0], inv_ref.shape[2]
    own = weight_ref.shape[1]
    half = own // 2
    nb = (n_rows - NC) // NI
    wst = st_src.shape[1]
    blk = 8 * n_sub

    barrier = pltpu.get_barrier_semaphore()

    @pl.loop(1, n_sub)
    def _(step):
        pl.semaphore_signal(barrier, inc=1, device_id={"sub": lax.rem(me + step, n_sub)})

    @pl.loop(1, n_cl)
    def _(step):
        pl.semaphore_signal(barrier, inc=1, device_id={"cluster": lax.rem(cl + step, n_cl)})

    fields = (
        (loads_hbm, loads_t), (basis_hbm, basis_ref), (scale_hbm, scale_ref), (inv_hbm, inv_ref),
        (corner_hbm, corner_ref), (weight_hbm, weight_ref), (iface_hbm, iface_ref),
        (glue_hbm, glue_ref), (s_hbm, smat),
    )
    copies = [pltpu.make_async_copy(a, b, load_sem.at[i]) for i, (a, b) in enumerate(fields)]
    for copy in copies:
        copy.start()

    def spread(src_of, buf, sem, axis, here, n, rows=8):
        @pl.loop(0, n - 1)
        def _(i):
            sign = 1 - 2 * lax.rem(i, 2)
            peer = lax.rem(here + n // 2 + sign * lax.div(i + 1, 2), n)
            pltpu.make_async_remote_copy(
                src_ref=src_of(peer).at[pl.ds(0, rows)],
                dst_ref=buf.at[here, pl.ds(0, rows)],
                send_sem=sem.at[0],
                recv_sem=sem.at[1],
                device_id={axis: peer},
            ).start()

    def drain(buf, sem, which, n, rows=8):
        view = buf.at[pl.ds(0, n - 1), pl.ds(0, rows)]
        pltpu.make_async_copy(view, view, sem.at[which]).wait()

    for copy in copies[:-1]:
        copy.wait()
    basis8 = jnp.concatenate([basis_ref[i] for i in range(nz)] + [jnp.zeros((8 - nz, n_rows), f32)], axis=0)
    b8[...] = split_rows(basis8)
    high, low = split(basis8)
    high, low = high.astype(f32), low.astype(f32)
    cols = jnp.transpose(
        jnp.concatenate([high, high, low, jnp.broadcast_to(scale_ref[...], (8, n_rows))], axis=0)
    )
    bt[...] = cols.astype(bf16)
    dmat[...] = jnp.broadcast_to(cols[:, 24:25], (n_rows, r_cols))

    corner_row = corner_ref[...]
    eye = iota((NC, NC), 0) == iota((NC, NC), 1)
    ccol[...] = jnp.sum(jnp.where(eye, corner_row, 0), axis=1, keepdims=True).astype(f32)
    corner_col = ccol[...].astype(jnp.int32)

    m = iota((blk, NC), 0)
    base = (m >> 3) * own + (m & 7)
    first, second = (base == corner_row).astype(f32), (base + half == corner_row).astype(f32)
    oh[...] = jnp.concatenate([first, second, first, second], axis=1).astype(bf16)
    m = iota((NC, blk), 1)
    base = (m >> 3) * own + (m & 7)
    pick = jnp.concatenate([base == corner_col, base + half == corner_col], axis=0)
    pick = pick.astype(f32).astype(bf16)
    ohT[...] = jnp.concatenate([pick, pick], axis=1)

    st_src[...] = jnp.zeros(st_src.shape, f32)
    for i in range(nz):
        st_src[i:i + 1, 0:cm] = inv_ref[i]
    st_src[0:nz, wst - NC:wst] = basis8[0:nz, 0:NC]
    st_src[nz:nz + 1, wst - NC:wst] = scale_ref[:, 0:NC]
    st_src[nz + 1:nz + 2, wst - NC:wst] = corner_row.astype(f32)
    st_src[nz + 1:nz + 2, 0:own] = weight_ref[...]

    ea, eb = iota((wst, blk), 0), iota((wst, blk), 1)
    grow[...] = (
        ((ea == (eb >> 3) * nz + (eb & 7)) & ((eb & 7) < nz) & (ea < cm)).astype(f32).astype(bf16)
    )
    row_ok = iota((8, wst), 0) < nz
    inv_own[...] = mm(split_rows(jnp.where(row_ok, st_src[...], 0.0)), grow[...]).astype(bf16)

    def packed_corners(v):
        zero = jnp.zeros((NC, r_cols), f32)
        parts = []
        for x in split(v):
            x = x.astype(f32)
            parts += [jnp.concatenate([x, zero], axis=1), jnp.concatenate([zero, x], axis=1)]
        return mm(oh[...], jnp.concatenate(parts, axis=0).astype(bf16))

    def basis_t(e):
        high, low = split(e)
        high, low = high.astype(f32), low.astype(f32)
        stack = jnp.concatenate([high, low, high, jnp.zeros((8, r_cols), f32)], axis=0)
        return mm(bt[...], stack.astype(bf16))

    tail = jnp.zeros((3, r_cols), f32)

    def first_message(k, vec, sums):
        pieces = halves_dot(b8[...], vec)
        sums = list(sums) + [jnp.zeros((1, r_cols), f32)] * (4 - len(sums))
        msg = jnp.concatenate(
            [
                jnp.concatenate([pieces[0:3], sums[0], sums[1], tail], axis=0),
                jnp.concatenate([pieces[3:6], sums[2], sums[3], tail], axis=0),
            ],
            axis=1,
        )
        p1_src[k] = msg
        p1_buf[k, me] = msg

    def send_first(k):
        spread(lambda peer: p1_src.at[k], p1_buf.at[k], p1_sem.at[k], "sub", me, n_sub, 5)

    def first_received(k):
        drain(p1_buf.at[k], p1_sem.at[k], 1, n_sub, 5)
        got = p1_buf[k]
        at = iota(got.shape, 1)
        got = jnp.where(at < 5, got, 0.0)
        moved = pltpu.roll(pltpu.roll(got, r_cols, 2), 3, 1)
        pieces = jnp.where(at < 3, got, jnp.where(at < nz, moved, 0.0))
        return pieces.reshape(blk, 2 * r_cols)[:, 0:r_cols], jnp.sum(got, axis=0)[3:5]

    def corner_message(k, vec):
        rs_src[k] = packed_corners(vec).reshape(n_sub, 8, 2 * r_cols)
        rs_buf[k, me] = rs_src[k, me]

    def send_corners(k):
        spread(lambda peer: rs_src.at[k, peer], rs_buf.at[k], rs_sem.at[k], "sub", me, n_sub)

    def own_corners(k):
        drain(rs_buf.at[k], rs_sem.at[k], 1, n_sub)
        total = jnp.sum(rs_buf[k], axis=0)
        ag_src[k] = total
        ag_buf[k, me] = total
        spread(lambda peer: ag_src.at[k], ag_buf.at[k], ag_sem.at[k], "sub", me, n_sub)

    def corner_back(k):
        drain(ag_buf.at[k], ag_sem.at[k], 1, n_sub)
        got = ag_buf[k].reshape(blk, 2 * r_cols)
        high, low = split(got)
        quad = mm(ohT[...], jnp.concatenate([high, low], axis=0))
        return quad[0:NC, 0:r_cols] + quad[NC:2 * NC, r_cols:2 * r_cols]

    glue_here = glue_ref[...].astype(f32)
    hi = NI // 2

    def placed(side, b):
        return (iface_ref[0:1, 1 - side:2 - side] == b).astype(f32)

    def block_of(side, ref):
        rows = jnp.zeros((NI, r_cols), f32)
        for b in range(nb):
            rows = rows + placed(side, b) * ref[NC + b * NI:NC + (b + 1) * NI, :]
        return rows

    def send_glue(k, ref):
        for side in range(2):
            rows = block_of(side, ref)
            gl_src[k, side, 0:hi, :] = jnp.concatenate([rows[0:hi], rows[hi:NI]], axis=1)
            gl_src[k, side, hi:hi + 8, :] = jnp.broadcast_to(glue_here, (8, 2 * r_cols))
        for side, peer in ((0, lax.rem(cl + 1, n_cl)), (1, lax.rem(cl + n_cl - 1, n_cl))):
            pltpu.make_async_remote_copy(
                src_ref=gl_src.at[k, side],
                dst_ref=gl_buf.at[k, side],
                send_sem=gl_sem.at[k, side, 0],
                recv_sem=gl_sem.at[k, side, 1],
                device_id={"cluster": peer},
            ).start()

    def glue_wait(k, which):
        for side in range(2):
            pltpu.make_async_copy(
                gl_src.at[k, side], gl_buf.at[k, side], gl_sem.at[k, side, which]
            ).wait()

    def unpack(k, side):
        a = gl_buf[k, side, 0:hi, :]
        return jnp.concatenate([a[:, 0:r_cols], a[:, r_cols:2 * r_cols]], axis=0)

    def spread_static():
        @pl.loop(1, n_sub // 2)
        def _(i):
            pltpu.make_async_remote_copy(
                src_ref=st_src,
                dst_ref=st_buf.at[core, place],
                send_sem=st_sem.at[0],
                recv_sem=st_sem.at[1],
                device_id={"sub": lax.rem(me + 2 * i, n_sub)},
            ).start()

    def pair_static():
        view = st_buf.at[0, pl.ds(0, n_sub // 2 - 1)]
        pltpu.make_async_copy(view, view, st_sem.at[1]).wait()
        pltpu.make_async_remote_copy(
            src_ref=st_buf.at[core],
            dst_ref=st_buf.at[core],
            send_sem=st_sem.at[2],
            recv_sem=st_sem.at[3],
            device_id={"sub": me + 1 - 2 * core},
        ).start()

    lv[...] = jnp.transpose(loads_t[...])
    loads = lv[...]
    scaled = dmat[...] * loads
    corner_message(0, scaled[0:NC, :])
    first_message(0, loads, [jnp.sum(scaled * loads, axis=0, keepdims=True)])
    core, place = lax.rem(me, 2), lax.div(me, 2)
    st_buf[core, place] = st_src[...]

    pl.semaphore_wait(barrier, n_sub + n_cl - 2)

    send_corners(0)
    send_first(0)
    spread_static()
    copies[-1].wait()
    own_corners(0)
    first_pieces, first_sums = first_received(0)
    z = dmat[...] * lv[...] + basis_t(halves_dot(inv_own[...], first_pieces))
    zv[...] = z
    dv[...] = z

    def product(k, last):
        half_d = dv[...].astype(bf16)
        top = jnp.dot(smat[0:NC, :], half_d, preferred_element_type=f32)
        sv[0:NC, :] = top
        if not last:
            corner_message(k + 1, dmat[0:NC, :] * top)
            send_corners(k + 1)
        if k == 0:
            send_glue(0, zv)
        sv[NC:, :] = jnp.dot(smat[NC:, :], half_d, preferred_element_type=f32)

    product(0, False)

    lane = iota((NC, NC), 1).astype(f32)
    row_ok = (iota((8, wst), 0) < nz) & (iota((8, wst), 1) < cm)
    n_half = n_sub // 2

    def tables(side, ws, srow):
        stack = []
        for i in range(n_half):
            slot = st_buf[side, i]
            tile = slot[:, wst - NC:wst]
            match = (ccol[...] == tile[nz + 1:nz + 2, :]).astype(f32).astype(bf16)
            both = mm(split_rows(tile), match, ((1,), (1,)))
            rows = both[0:8] + both[8:16]
            s = 2 * i + side
            ct[pl.ds(pl.multiple_of(8 * s, 8), 8), :] = rows
            srow = srow + rows[nz:nz + 1, :]
            mine = (ccol[...] - (s * own).astype(f32) == lane) & (lane < own)
            ws = ws + jnp.where(mine, slot[nz + 1:nz + 2, 0:NC], 0.0)
            stack.append(jnp.where(row_ok, slot, 0.0))
        both = mm(split_rows(jnp.concatenate(stack, axis=0)), grow[...])
        for i in range(n_half):
            row = pl.multiple_of(8 * (2 * i + side), 8)
            wide[pl.ds(row, 8), :] = both[8 * i:8 * i + 8]
            wide[pl.ds(blk + row, 8), :] = both[8 * (n_half + i):8 * (n_half + i) + 8]
        return ws, srow

    pair_static()
    ws, srow = tables(core, jnp.zeros((NC, NC), f32), jnp.zeros((1, NC), f32))
    pltpu.make_async_copy(st_buf.at[0], st_buf.at[0], st_sem.at[3]).wait()
    ws, srow = tables(1 - core, ws, srow)
    wcol[...] = jnp.sum(ws, axis=1, keepdims=True)
    scol[...] = jnp.sum(jnp.where(eye, srow, 0.0), axis=1, keepdims=True) * wcol[...]
    ctt[...] = split_rows(jnp.transpose(ct[...]))
    invx[...] = wide[...].astype(bf16)

    def coarse(pieces):
        e_all = halves_dot(invx[...], pieces)
        e_scr[...] = e_all
        return jnp.sum(pieces * e_all, axis=0, keepdims=True)

    rho_part = first_sums[0:1, 0:r_cols] + coarse(first_pieces)
    tz[...] = corner_back(0) + halves_dot(ctt[...], e_scr[...])
    td[...] = tz[...]
    xv[...] = jnp.zeros_like(xv)

    def finish_product(k, step, beta):
        sv[0:NC, :] = sv[0:NC, :] + wcol[...] * td[...]
        glue_wait(k, 1)
        if k == 0:
            nlz[...] = unpack(k, 1)
            prz[...] = unpack(k, 0)
            nld[...] = nlz[...]
            prd[...] = prz[...]
        else:
            nlz[...] = nlz[...] - step * unpack(k, 1)
            prz[...] = prz[...] - step * unpack(k, 0)
            nld[...] = nlz[...] + beta * nld[...]
            prd[...] = prz[...] + beta * prd[...]
        prev_glue = gl_buf[0, 0, hi:hi + 1, 0:r_cols]
        jump_right = glue_here * (block_of(0, dv) - nld[...])
        jump_left = prev_glue * (prd[...] - block_of(1, dv))
        for b in range(nb):
            rows = slice(NC + b * NI, NC + (b + 1) * NI)
            sv[rows, :] = sv[rows, :] + placed(0, b) * jump_right - placed(1, b) * jump_left

    rho = step = beta = None
    for k in range(ITERS):
        last = k + 1 == ITERS
        finish_product(k, step, beta)
        s, d = sv[...], dv[...]
        curve_part = jnp.sum(d * s, axis=0, keepdims=True)
        if not last:
            ds = dmat[...] * s
            sums = [
                curve_part,
                jnp.sum(zv[...] * s, axis=0, keepdims=True),
                jnp.sum(ds * s, axis=0, keepdims=True),
            ]
            first_message(k + 1, s, sums)
            send_first(k + 1)
            own_corners(k + 1)
            pieces, sums = first_received(k + 1)
            quad = coarse(pieces)
            parts = [sums[0:1, 0:r_cols], sums[1:2, 0:r_cols], sums[0:1, r_cols:] + quad]
        else:
            msg = jnp.concatenate([curve_part, curve_part], axis=1)
            p1_src[k + 1, 0:1] = msg
            p1_buf[k + 1, me, 0:1] = msg
            spread(lambda peer: p1_src.at[k + 1], p1_buf.at[k + 1], p1_sem.at[k + 1],
                   "sub", me, n_sub, 1)
            drain(p1_buf.at[k + 1], p1_sem.at[k + 1], 1, n_sub, 1)
            sums = jnp.sum(p1_buf[k + 1, :, 0:1], axis=0)[:, 0:r_cols]
            parts = [sums, sums, sums]
        msg = jnp.concatenate(
            [
                jnp.concatenate([parts[0], parts[1]], axis=1),
                jnp.concatenate([parts[2], rho_part], axis=1),
            ],
            axis=0,
        )
        p2_src[k] = msg
        p2_buf[k, cl] = msg
        spread(lambda peer: p2_src.at[k], p2_buf.at[k], p2_sem.at[k], "cluster", cl, n_cl, 2)
        if not last:
            e_own = e_scr[pl.ds(8 * me, 8), :]
            qv[...] = ds + basis_t(e_own)
            send_glue(k + 1, qv)
            tq[...] = scol[...] * td[...] + halves_dot(ctt[...], e_scr[...])
        drain(p2_buf.at[k], p2_sem.at[k], 1, n_cl, 2)
        total = jnp.sum(p2_buf[k], axis=0)
        curve = total[0:1, 0:r_cols]
        if k == 0:
            rho = total[1:2, r_cols:2 * r_cols]
        step = rho / curve
        if last:
            out_ref[...] = xv[...] + step * dv[...]
            break
        zs = total[0:1, r_cols:2 * r_cols]
        sq = total[1:2, 0:r_cols]
        rho_next = rho - 2.0 * step * zs + step * (step * sq)
        beta = rho_next / rho
        d = dv[...]
        z = zv[...] - step * qv[...]
        zv[...] = z
        dv[...] = z + beta * d
        xv[...] = xv[...] + step * d
        rho = rho_next
        product(k + 1, k + 2 == ITERS)
        tz[...] = tz[...] - step * (tq[...] + corner_back(k + 1))
        td[...] = tz[...] + beta * td[...]

    view = st_buf.at[0, pl.ds(0, n_sub // 2 - 1)]
    pltpu.make_async_copy(view, view, st_sem.at[0]).wait()
    pltpu.make_async_copy(st_buf.at[0], st_buf.at[0], st_sem.at[2]).wait()
    for k in range(ITERS + 1):
        drain(p1_buf.at[k], p1_sem.at[k], 0, n_sub, 5 if k < ITERS else 1)
    for k in range(ITERS):
        drain(rs_buf.at[k], rs_sem.at[k], 0, n_sub)
        drain(ag_buf.at[k], ag_sem.at[k], 0, n_sub)
        drain(p2_buf.at[k], p2_sem.at[k], 0, n_cl, 2)
        glue_wait(k, 0)


def per_device(
    n_sub, n_cl, schur_block, load_cases, precond_scale, coarse_basis, coarse_inverse,
    corner_weight, corner_index, iface_block, glue_link,
):
    n_rows, r = load_cases.shape[2:]
    nz, cm = coarse_basis.shape[2], coarse_inverse.shape[2]
    blk = 8 * n_sub
    wst = -(-(cm + NC) // 128) * 128
    vec = pltpu.VMEM((n_rows, r), f32)
    vmem = pl.BlockSpec(memory_space=pltpu.VMEM)
    hbm = pl.BlockSpec(memory_space=pltpu.HBM)
    own = corner_weight.shape[1]
    dma = pltpu.SemaphoreType.DMA
    operands = (
        schur_block[0, 0], load_cases[0, 0].T, precond_scale[0],
        jnp.swapaxes(coarse_basis[0], 0, 1), jnp.swapaxes(coarse_inverse, 0, 1),
        corner_weight, corner_index[0], iface_block[0],
    )
    out = pl.pallas_call(
        functools.partial(kernel, n_sub, n_cl),
        out_shape=jax.ShapeDtypeStruct((n_rows, r), f32),
        in_specs=[hbm] * 9,
        out_specs=vmem,
        scratch_shapes=[
            pltpu.VMEM((n_rows, n_rows), bf16),
            pltpu.VMEM((r, n_rows), f32),
            pltpu.VMEM((1, n_rows), f32),
            pltpu.VMEM((nz, 1, n_rows), f32),
            pltpu.VMEM((nz, 1, cm), f32),
            pltpu.VMEM((1, own), f32),
            pltpu.VMEM((1, NC), jnp.int32),
            pltpu.VMEM((1, 2), jnp.int32),
            pltpu.VMEM((1, 1), jnp.int32),
            vec,
            pltpu.VMEM((NI, r), f32),
            pltpu.VMEM((NI, r), f32),
            pltpu.VMEM((NI, r), f32),
            pltpu.VMEM((NI, r), f32),
            pltpu.VMEM((NC, 1), f32),
            pltpu.VMEM((16, n_rows), bf16),
            pltpu.VMEM((n_rows, 32), bf16),
            vec, vec, vec, vec, vec, vec,
            pltpu.VMEM((2 * NC, 2 * blk), bf16),
            pltpu.VMEM((blk, 4 * NC), bf16),
            pltpu.VMEM((blk, NC), f32),
            pltpu.VMEM((2 * NC, blk), bf16),
            pltpu.VMEM((2 * blk, blk), f32),
            pltpu.VMEM((2 * blk, blk), bf16),
            pltpu.VMEM((16, blk), bf16),
            pltpu.VMEM((wst, blk), bf16),
            pltpu.VMEM((blk, r), f32),
            pltpu.VMEM((NC, 1), f32),
            pltpu.VMEM((NC, 1), f32),
            pltpu.VMEM((8, wst), f32),
            pltpu.VMEM((2, n_sub // 2, 8, wst), f32),
            pltpu.VMEM((ITERS + 1, 8, 2 * r), f32),
            pltpu.VMEM((ITERS + 1, n_sub, 8, 2 * r), f32),
            pltpu.VMEM((ITERS, n_sub, 8, 2 * r), f32),
            pltpu.VMEM((ITERS, n_sub, 8, 2 * r), f32),
            pltpu.VMEM((ITERS, 8, 2 * r), f32),
            pltpu.VMEM((ITERS, n_sub, 8, 2 * r), f32),
            pltpu.VMEM((ITERS, 2, 2 * r), f32),
            pltpu.VMEM((ITERS, n_cl, 2, 2 * r), f32),
            pltpu.VMEM((ITERS, 2, NI // 2 + 8, 2 * r), f32),
            pltpu.VMEM((ITERS, 2, NI // 2 + 8, 2 * r), f32),
            pltpu.VMEM((NC, r), f32),
            pltpu.VMEM((NC, r), f32),
            pltpu.VMEM((NC, r), f32),
            dma((9,)),
            dma((4,)),
            dma((ITERS + 1, 2)),
            dma((ITERS, 2)),
            dma((ITERS, 2)),
            dma((ITERS, 2)),
            dma((ITERS, 2, 2)),
        ],
        compiler_params=pltpu.CompilerParams(
            collective_id=0, has_side_effects=True, vmem_limit_bytes=40 * 1024 * 1024
        ),
    )(
        *(pltpu.with_memory_space_constraint(a, pltpu.HBM) for a in operands), glue_link,
    )
    return out[None, None]


def solution(mesh):
    in_specs = (
        P("cluster", "sub", None, None),
        P("cluster", "sub", None, None),
        P("cluster", "sub", None),
        P("cluster", "sub", None, None),
        P("cluster", "sub", None),
        P("cluster", "sub"),
        P("cluster", "sub", None),
        P("cluster", "sub", None),
        P("cluster", "sub"),
    )
    return jax.shard_map(
        functools.partial(per_device, mesh.shape["sub"], mesh.shape["cluster"]),
        mesh=mesh, in_specs=in_specs, out_specs=P("cluster", "sub", None, None), check_vma=False,
    )
```

```python
import functools

import jax
import jax.numpy as jnp
from jax import lax
from jax.experimental import pallas as pl
from jax.experimental.pallas import tpu as pltpu
from jax.sharding import PartitionSpec as P

NC = 64
NI = 128
ITERS = 3
f32 = jnp.float32
bf16 = jnp.bfloat16


def mm(a, b, dims=((1,), (0,))):
    return lax.dot_general(a, b, (dims, ((), ())), preferred_element_type=f32)


def split(x):
    high = x.astype(bf16)
    return high, (x - high.astype(f32)).astype(bf16)


def split_rows(x):
    high, low = split(x)
    return jnp.concatenate([high.astype(f32), low.astype(f32)], axis=0).astype(bf16)


def halves_dot(pair, x):
    n = pair.shape[0] // 2
    high, low = split(x)
    both = mm(pair, high)
    return both[0:n] + both[n:2 * n] + mm(pair[0:n], low)


def iota(shape, dim):
    return lax.broadcasted_iota(jnp.int32, shape, dim)


def kernel(
    n_sub, n_cl,
    s_hbm, loads_hbm, scale_hbm, basis_hbm, inv_hbm, weight_hbm, corner_hbm, iface_hbm, glue_hbm,
    out_ref,
    smat, loads_t, scale_ref, basis_ref, inv_ref, weight_ref, corner_ref, iface_ref, glue_ref,
    lv, nld, prd, nlz, prz, scol,
    b8, bt, dmat, zv, dv, xv, sv, qv,
    ohT, oh, ct, ctt, wide, invx, inv_own, grow, e_scr, ccol, wcol,
    st_src, st_buf,
    p1_src, p1_buf, rs_src, rs_buf, ag_src, ag_buf, p2_src, p2_buf, gl_src, gl_buf,
    tq, td, tz,
    load_sem, st_sem, p1_sem, rs_sem, ag_sem, p2_sem, gl_sem,
):
    me = lax.axis_index("sub")
    cl = lax.axis_index("cluster")
    r_cols, n_rows = loads_t.shape
    nz, cm = basis_ref.shape[0], inv_ref.shape[2]
    own = weight_ref.shape[1]
    half = own // 2
    nb = (n_rows - NC) // NI
    wst = st_src.shape[1]
    blk = 8 * n_sub

    barrier = pltpu.get_barrier_semaphore()

    @pl.loop(1, n_sub)
    def _(step):
        pl.semaphore_signal(barrier, inc=1, device_id={"sub": lax.rem(me + step, n_sub)})

    @pl.loop(1, n_cl)
    def _(step):
        pl.semaphore_signal(barrier, inc=1, device_id={"cluster": lax.rem(cl + step, n_cl)})

    fields = (
        (loads_hbm, loads_t), (basis_hbm, basis_ref), (scale_hbm, scale_ref), (inv_hbm, inv_ref),
        (corner_hbm, corner_ref), (weight_hbm, weight_ref), (iface_hbm, iface_ref),
        (glue_hbm, glue_ref), (s_hbm, smat),
    )
    copies = [pltpu.make_async_copy(a, b, load_sem.at[i]) for i, (a, b) in enumerate(fields)]
    for copy in copies:
        copy.start()

    def spread(src_of, buf, sem, axis, here, n, rows=8):
        @pl.loop(0, n - 1)
        def _(i):
            sign = 1 - 2 * lax.rem(i, 2)
            peer = lax.rem(here + n // 2 + sign * lax.div(i + 1, 2), n)
            pltpu.make_async_remote_copy(
                src_ref=src_of(peer).at[pl.ds(0, rows)],
                dst_ref=buf.at[here, pl.ds(0, rows)],
                send_sem=sem.at[0],
                recv_sem=sem.at[1],
                device_id={axis: peer},
            ).start()

    def drain(buf, sem, which, n, rows=8):
        view = buf.at[pl.ds(0, n - 1), pl.ds(0, rows)]
        pltpu.make_async_copy(view, view, sem.at[which]).wait()

    for copy in copies[:-1]:
        copy.wait()
    basis8 = jnp.concatenate([basis_ref[i] for i in range(nz)] + [jnp.zeros((8 - nz, n_rows), f32)], axis=0)
    b8[...] = split_rows(basis8)
    high, low = split(basis8)
    high, low = high.astype(f32), low.astype(f32)
    cols = jnp.transpose(
        jnp.concatenate([high, high, low, jnp.broadcast_to(scale_ref[...], (8, n_rows))], axis=0)
    )
    bt[...] = cols.astype(bf16)
    dmat[...] = jnp.broadcast_to(cols[:, 24:25], (n_rows, r_cols))

    corner_row = corner_ref[...]
    eye = iota((NC, NC), 0) == iota((NC, NC), 1)
    ccol[...] = jnp.sum(jnp.where(eye, corner_row, 0), axis=1, keepdims=True).astype(f32)
    corner_col = ccol[...].astype(jnp.int32)

    m = iota((blk, NC), 0)
    base = (m >> 3) * own + (m & 7)
    first, second = (base == corner_row).astype(f32), (base + half == corner_row).astype(f32)
    oh[...] = jnp.concatenate([first, second, first, second], axis=1).astype(bf16)
    m = iota((NC, blk), 1)
    base = (m >> 3) * own + (m & 7)
    pick = jnp.concatenate([base == corner_col, base + half == corner_col], axis=0)
    pick = pick.astype(f32).astype(bf16)
    ohT[...] = jnp.concatenate([pick, pick], axis=1)

    st_src[...] = jnp.zeros(st_src.shape, f32)
    for i in range(nz):
        st_src[i:i + 1, 0:cm] = inv_ref[i]
    st_src[0:nz, wst - NC:wst] = basis8[0:nz, 0:NC]
    st_src[nz:nz + 1, wst - NC:wst] = scale_ref[:, 0:NC]
    st_src[nz:nz + 1, NC:2 * NC] = corner_row.astype(f32)
    st_src[nz:nz + 1, 0:own] = weight_ref[...]

    ea, eb = iota((wst, blk), 0), iota((wst, blk), 1)
    grow[...] = (
        ((ea == (eb >> 3) * nz + (eb & 7)) & ((eb & 7) < nz) & (ea < cm)).astype(f32).astype(bf16)
    )
    row_ok = iota((8, wst), 0) < nz
    inv_own[...] = mm(split_rows(jnp.where(row_ok, st_src[...], 0.0)), grow[...]).astype(bf16)

    def packed_corners(v):
        zero = jnp.zeros((NC, r_cols), f32)
        parts = []
        for x in split(v):
            x = x.astype(f32)
            parts += [jnp.concatenate([x, zero], axis=1), jnp.concatenate([zero, x], axis=1)]
        return mm(oh[...], jnp.concatenate(parts, axis=0).astype(bf16))

    def basis_t(e):
        high, low = split(e)
        high, low = high.astype(f32), low.astype(f32)
        stack = jnp.concatenate([high, low, high, jnp.zeros((8, r_cols), f32)], axis=0)
        return mm(bt[...], stack.astype(bf16))

    tail = jnp.zeros((3, r_cols), f32)

    def first_message(k, vec, sums):
        pieces = halves_dot(b8[...], vec)
        sums = list(sums) + [jnp.zeros((1, r_cols), f32)] * (4 - len(sums))
        msg = jnp.concatenate(
            [
                jnp.concatenate([pieces[0:3], sums[0], sums[1], tail], axis=0),
                jnp.concatenate([pieces[3:6], sums[2], sums[3], tail], axis=0),
            ],
            axis=1,
        )
        p1_src[k] = msg
        p1_buf[k, me] = msg

    def send_first(k):
        spread(lambda peer: p1_src.at[k], p1_buf.at[k], p1_sem.at[k], "sub", me, n_sub, 5)

    def first_received(k):
        drain(p1_buf.at[k], p1_sem.at[k], 1, n_sub, 5)
        got = p1_buf[k]
        at = iota(got.shape, 1)
        got = jnp.where(at < 5, got, 0.0)
        moved = pltpu.roll(pltpu.roll(got, r_cols, 2), 3, 1)
        pieces = jnp.where(at < 3, got, jnp.where(at < nz, moved, 0.0))
        return pieces.reshape(blk, 2 * r_cols)[:, 0:r_cols], jnp.sum(got, axis=0)[3:5]

    def corner_message(k, vec):
        rs_src[k] = packed_corners(vec).reshape(n_sub, 8, 2 * r_cols)
        rs_buf[k, me] = rs_src[k, me]

    def send_corners(k):
        spread(lambda peer: rs_src.at[k, peer], rs_buf.at[k], rs_sem.at[k], "sub", me, n_sub)

    def own_corners(k):
        drain(rs_buf.at[k], rs_sem.at[k], 1, n_sub)
        total = jnp.sum(rs_buf[k], axis=0)
        ag_src[k] = total
        ag_buf[k, me] = total
        spread(lambda peer: ag_src.at[k], ag_buf.at[k], ag_sem.at[k], "sub", me, n_sub)

    def corner_back(k):
        drain(ag_buf.at[k], ag_sem.at[k], 1, n_sub)
        got = ag_buf[k].reshape(blk, 2 * r_cols)
        high, low = split(got)
        quad = mm(ohT[...], jnp.concatenate([high, low], axis=0))
        return quad[0:NC, 0:r_cols] + quad[NC:2 * NC, r_cols:2 * r_cols]

    glue_here = glue_ref[...].astype(f32)
    hi = NI // 2

    def placed(side, b):
        return (iface_ref[0:1, 1 - side:2 - side] == b).astype(f32)

    def block_of(side, ref):
        rows = jnp.zeros((NI, r_cols), f32)
        for b in range(nb):
            rows = rows + placed(side, b) * ref[NC + b * NI:NC + (b + 1) * NI, :]
        return rows

    def send_glue(k, ref):
        for side in range(2):
            rows = block_of(side, ref)
            gl_src[k, side, 0:hi, :] = jnp.concatenate([rows[0:hi], rows[hi:NI]], axis=1)
            gl_src[k, side, hi:hi + 8, :] = jnp.broadcast_to(glue_here, (8, 2 * r_cols))
        for side, peer in ((0, lax.rem(cl + 1, n_cl)), (1, lax.rem(cl + n_cl - 1, n_cl))):
            pltpu.make_async_remote_copy(
                src_ref=gl_src.at[k, side],
                dst_ref=gl_buf.at[k, side],
                send_sem=gl_sem.at[k, side, 0],
                recv_sem=gl_sem.at[k, side, 1],
                device_id={"cluster": peer},
            ).start()

    def glue_wait(k, which):
        for side in range(2):
            pltpu.make_async_copy(
                gl_src.at[k, side], gl_buf.at[k, side], gl_sem.at[k, side, which]
            ).wait()

    def unpack(k, side):
        a = gl_buf[k, side, 0:hi, :]
        return jnp.concatenate([a[:, 0:r_cols], a[:, r_cols:2 * r_cols]], axis=0)

    def spread_static():
        @pl.loop(1, n_sub // 2)
        def _(i):
            pltpu.make_async_remote_copy(
                src_ref=st_src.at[pl.ds(0, 7)],
                dst_ref=st_buf.at[core, place, pl.ds(0, 7)],
                send_sem=st_sem.at[0],
                recv_sem=st_sem.at[1],
                device_id={"sub": lax.rem(me + 2 * i, n_sub)},
            ).start()

    def pair_static():
        view = st_buf.at[0, pl.ds(0, n_sub // 2 - 1), pl.ds(0, 7)]
        pltpu.make_async_copy(view, view, st_sem.at[1]).wait()
        pltpu.make_async_remote_copy(
            src_ref=st_buf.at[core, :, pl.ds(0, 7)],
            dst_ref=st_buf.at[core, :, pl.ds(0, 7)],
            send_sem=st_sem.at[2],
            recv_sem=st_sem.at[3],
            device_id={"sub": me + 1 - 2 * core},
        ).start()

    lv[...] = jnp.transpose(loads_t[...])
    loads = lv[...]
    scaled = dmat[...] * loads
    corner_message(0, scaled[0:NC, :])
    first_message(0, loads, [jnp.sum(scaled * loads, axis=0, keepdims=True)])
    core, place = lax.rem(me, 2), lax.div(me, 2)
    st_buf[core, place] = st_src[...]

    pl.semaphore_wait(barrier, n_sub + n_cl - 2)

    send_corners(0)
    send_first(0)
    spread_static()
    copies[-1].wait()
    own_corners(0)
    first_pieces, first_sums = first_received(0)
    z = dmat[...] * lv[...] + basis_t(halves_dot(inv_own[...], first_pieces))
    zv[...] = z
    dv[...] = z

    def jumps(k, step, beta):
        glue_wait(k, 1)
        if k == 0:
            nlz[...] = unpack(k, 1)
            prz[...] = unpack(k, 0)
            nld[...] = nlz[...]
            prd[...] = prz[...]
        else:
            nlz[...] = nlz[...] - step * unpack(k, 1)
            prz[...] = prz[...] - step * unpack(k, 0)
            nld[...] = nlz[...] + beta * nld[...]
            prd[...] = prz[...] + beta * prd[...]
        prev_glue = gl_buf[0, 0, hi:hi + 1, 0:r_cols]
        return glue_here * (block_of(0, dv) - nld[...]), prev_glue * (prd[...] - block_of(1, dv))

    def add_jumps(jump):
        for b in range(nb):
            rows = slice(NC + b * NI, NC + (b + 1) * NI)
            sv[rows, :] = sv[rows, :] + placed(0, b) * jump[0] - placed(1, b) * jump[1]

    def product(k, last, step, beta):
        half_d = dv[...].astype(bf16)
        top = mm(smat[0:NC, :], half_d)
        sv[0:NC, :] = top
        if not last:
            corner_message(k + 1, dmat[0:NC, :] * top)
        if k == 0:
            send_glue(0, zv)
        elif not last:
            send_corners(k + 1)
        if k > 0:
            jump = jumps(k, step, beta)
        sv[NC:, :] = mm(smat[NC:, :], half_d)
        if k > 0:
            add_jumps(jump)

    product(0, False, None, None)

    lane = iota((NC, NC), 1).astype(f32)
    row_ok = (iota((8, wst), 0) < nz) & (iota((8, wst), 1) < cm)
    tile_ok = iota((8, NC), 0) <= nz
    n_half = n_sub // 2

    def tables(side, ws, srow):
        stack = []
        for i in range(n_half):
            slot = st_buf[side, i]
            tile = jnp.where(tile_ok, slot[:, wst - NC:wst], 0.0)
            match = (ccol[...] == slot[nz:nz + 1, NC:2 * NC]).astype(f32).astype(bf16)
            both = mm(split_rows(tile), match, ((1,), (1,)))
            rows = both[0:8] + both[8:16]
            s = 2 * i + side
            ct[pl.ds(pl.multiple_of(8 * s, 8), 8), :] = rows
            srow = srow + rows[nz:nz + 1, :]
            mine = (ccol[...] - (s * own).astype(f32) == lane) & (lane < own)
            ws = ws + jnp.where(mine, slot[nz:nz + 1, 0:NC], 0.0)
            stack.append(jnp.where(row_ok, slot, 0.0))
        both = mm(split_rows(jnp.concatenate(stack, axis=0)), grow[...])
        for i in range(n_half):
            row = pl.multiple_of(8 * (2 * i + side), 8)
            wide[pl.ds(row, 8), :] = both[8 * i:8 * i + 8]
            wide[pl.ds(blk + row, 8), :] = both[8 * (n_half + i):8 * (n_half + i) + 8]
        return ws, srow

    pair_static()
    send_corners(1)
    ws, srow = tables(core, jnp.zeros((NC, NC), f32), jnp.zeros((1, NC), f32))
    view = st_buf.at[0, :, pl.ds(0, 7)]
    pltpu.make_async_copy(view, view, st_sem.at[3]).wait()
    ws, srow = tables(1 - core, ws, srow)
    wcol[...] = jnp.sum(ws, axis=1, keepdims=True)
    scol[...] = jnp.sum(jnp.where(eye, srow, 0.0), axis=1, keepdims=True) * wcol[...]
    ctt[...] = split_rows(jnp.transpose(ct[...]))
    invx[...] = wide[...].astype(bf16)

    def coarse(pieces):
        e_all = halves_dot(invx[...], pieces)
        e_scr[...] = e_all
        return jnp.sum(pieces * e_all, axis=0, keepdims=True)

    rho_part = first_sums[0:1, 0:r_cols] + coarse(first_pieces)
    tz[...] = corner_back(0) + halves_dot(ctt[...], e_scr[...])
    td[...] = tz[...]
    xv[...] = jnp.zeros_like(xv)

    rho = step = beta = None
    for k in range(ITERS):
        last = k + 1 == ITERS
        sv[0:NC, :] = sv[0:NC, :] + wcol[...] * td[...]
        if k == 0:
            add_jumps(jumps(0, None, None))
        s, d = sv[...], dv[...]
        curve_part = jnp.sum(d * s, axis=0, keepdims=True)
        if not last:
            ds = dmat[...] * s
            sums = [
                curve_part,
                jnp.sum(zv[...] * s, axis=0, keepdims=True),
                jnp.sum(ds * s, axis=0, keepdims=True),
            ]
            first_message(k + 1, s, sums)
            send_first(k + 1)
            own_corners(k + 1)
            pieces, sums = first_received(k + 1)
            quad = coarse(pieces)
            parts = [sums[0:1, 0:r_cols], sums[1:2, 0:r_cols], sums[0:1, r_cols:] + quad]
        else:
            msg = jnp.concatenate([curve_part, curve_part], axis=1)
            p1_src[k + 1, 0:1] = msg
            p1_buf[k + 1, me, 0:1] = msg
            spread(lambda peer: p1_src.at[k + 1], p1_buf.at[k + 1], p1_sem.at[k + 1],
                   "sub", me, n_sub, 1)
            drain(p1_buf.at[k + 1], p1_sem.at[k + 1], 1, n_sub, 1)
            sums = jnp.sum(p1_buf[k + 1, :, 0:1], axis=0)[:, 0:r_cols]
            parts = [sums, sums, sums]
        msg = jnp.concatenate(
            [
                jnp.concatenate([parts[0], parts[1]], axis=1),
                jnp.concatenate([parts[2], rho_part], axis=1),
            ],
            axis=0,
        )
        p2_src[k] = msg
        p2_buf[k, cl] = msg
        spread(lambda peer: p2_src.at[k], p2_buf.at[k], p2_sem.at[k], "cluster", cl, n_cl, 2)
        if not last:
            e_own = e_scr[pl.ds(8 * me, 8), :]
            qv[...] = ds + basis_t(e_own)
            send_glue(k + 1, qv)
            tq[...] = scol[...] * td[...] + halves_dot(ctt[...], e_scr[...])
        drain(p2_buf.at[k], p2_sem.at[k], 1, n_cl, 2)
        total = jnp.sum(p2_buf[k], axis=0)
        curve = total[0:1, 0:r_cols]
        if k == 0:
            rho = total[1:2, r_cols:2 * r_cols]
        step = rho / curve
        if last:
            out_ref[...] = xv[...] + step * dv[...]
            break
        zs = total[0:1, r_cols:2 * r_cols]
        sq = total[1:2, 0:r_cols]
        rho_next = rho - 2.0 * step * zs + step * (step * sq)
        beta = rho_next / rho
        d = dv[...]
        z = zv[...] - step * qv[...]
        zv[...] = z
        dv[...] = z + beta * d
        xv[...] = xv[...] + step * d
        rho = rho_next
        product(k + 1, k + 2 == ITERS, step, beta)
        tz[...] = tz[...] - step * (tq[...] + corner_back(k + 1))
        td[...] = tz[...] + beta * td[...]

    view = st_buf.at[0, pl.ds(0, n_sub // 2 - 1), pl.ds(0, 7)]
    pltpu.make_async_copy(view, view, st_sem.at[0]).wait()
    view = st_buf.at[0, :, pl.ds(0, 7)]
    pltpu.make_async_copy(view, view, st_sem.at[2]).wait()
    for k in range(ITERS + 1):
        drain(p1_buf.at[k], p1_sem.at[k], 0, n_sub, 5 if k < ITERS else 1)
    for k in range(ITERS):
        drain(rs_buf.at[k], rs_sem.at[k], 0, n_sub)
        drain(ag_buf.at[k], ag_sem.at[k], 0, n_sub)
        drain(p2_buf.at[k], p2_sem.at[k], 0, n_cl, 2)
        glue_wait(k, 0)


def per_device(
    n_sub, n_cl, schur_block, load_cases, precond_scale, coarse_basis, coarse_inverse,
    corner_weight, corner_index, iface_block, glue_link,
):
    n_rows, r = load_cases.shape[2:]
    nz, cm = coarse_basis.shape[2], coarse_inverse.shape[2]
    blk = 8 * n_sub
    wst = max(-(-(cm + NC) // 128) * 128, 4 * NC)
    vec = pltpu.VMEM((n_rows, r), f32)
    vmem = pl.BlockSpec(memory_space=pltpu.VMEM)
    hbm = pl.BlockSpec(memory_space=pltpu.HBM)
    own = corner_weight.shape[1]
    dma = pltpu.SemaphoreType.DMA
    operands = (
        schur_block[0, 0], load_cases[0, 0].T, precond_scale[0],
        jnp.swapaxes(coarse_basis[0], 0, 1), jnp.swapaxes(coarse_inverse, 0, 1),
        corner_weight, corner_index[0], iface_block[0],
    )
    out = pl.pallas_call(
        functools.partial(kernel, n_sub, n_cl),
        out_shape=jax.ShapeDtypeStruct((n_rows, r), f32),
        in_specs=[hbm] * 9,
        out_specs=vmem,
        scratch_shapes=[
            pltpu.VMEM((n_rows, n_rows), bf16),
            pltpu.VMEM((r, n_rows), f32),
            pltpu.VMEM((1, n_rows), f32),
            pltpu.VMEM((nz, 1, n_rows), f32),
            pltpu.VMEM((nz, 1, cm), f32),
            pltpu.VMEM((1, own), f32),
            pltpu.VMEM((1, NC), jnp.int32),
            pltpu.VMEM((1, 2), jnp.int32),
            pltpu.VMEM((1, 1), jnp.int32),
            vec,
            pltpu.VMEM((NI, r), f32),
            pltpu.VMEM((NI, r), f32),
            pltpu.VMEM((NI, r), f32),
            pltpu.VMEM((NI, r), f32),
            pltpu.VMEM((NC, 1), f32),
            pltpu.VMEM((16, n_rows), bf16),
            pltpu.VMEM((n_rows, 32), bf16),
            vec, vec, vec, vec, vec, vec,
            pltpu.VMEM((2 * NC, 2 * blk), bf16),
            pltpu.VMEM((blk, 4 * NC), bf16),
            pltpu.VMEM((blk, NC), f32),
            pltpu.VMEM((2 * NC, blk), bf16),
            pltpu.VMEM((2 * blk, blk), f32),
            pltpu.VMEM((2 * blk, blk), bf16),
            pltpu.VMEM((16, blk), bf16),
            pltpu.VMEM((wst, blk), bf16),
            pltpu.VMEM((blk, r), f32),
            pltpu.VMEM((NC, 1), f32),
            pltpu.VMEM((NC, 1), f32),
            pltpu.VMEM((8, wst), f32),
            pltpu.VMEM((2, n_sub // 2, 8, wst), f32),
            pltpu.VMEM((ITERS + 1, 8, 2 * r), f32),
            pltpu.VMEM((ITERS + 1, n_sub, 8, 2 * r), f32),
            pltpu.VMEM((ITERS, n_sub, 8, 2 * r), f32),
            pltpu.VMEM((ITERS, n_sub, 8, 2 * r), f32),
            pltpu.VMEM((ITERS, 8, 2 * r), f32),
            pltpu.VMEM((ITERS, n_sub, 8, 2 * r), f32),
            pltpu.VMEM((ITERS, 2, 2 * r), f32),
            pltpu.VMEM((ITERS, n_cl, 2, 2 * r), f32),
            pltpu.VMEM((ITERS, 2, NI // 2 + 8, 2 * r), f32),
            pltpu.VMEM((ITERS, 2, NI // 2 + 8, 2 * r), f32),
            pltpu.VMEM((NC, r), f32),
            pltpu.VMEM((NC, r), f32),
            pltpu.VMEM((NC, r), f32),
            dma((9,)),
            dma((4,)),
            dma((ITERS + 1, 2)),
            dma((ITERS, 2)),
            dma((ITERS, 2)),
            dma((ITERS, 2)),
            dma((ITERS, 2, 2)),
        ],
        compiler_params=pltpu.CompilerParams(
            collective_id=0, has_side_effects=True, vmem_limit_bytes=40 * 1024 * 1024
        ),
    )(
        *(pltpu.with_memory_space_constraint(a, pltpu.HBM) for a in operands), glue_link,
    )
    return out[None, None]


def solution(mesh):
    in_specs = (
        P("cluster", "sub", None, None),
        P("cluster", "sub", None, None),
        P("cluster", "sub", None),
        P("cluster", "sub", None, None),
        P("cluster", "sub", None),
        P("cluster", "sub"),
        P("cluster", "sub", None),
        P("cluster", "sub", None),
        P("cluster", "sub"),
    )
    return jax.shard_map(
        functools.partial(per_device, mesh.shape["sub"], mesh.shape["cluster"]),
        mesh=mesh, in_specs=in_specs, out_specs=P("cluster", "sub", None, None), check_vma=False,
    )
```

```python
import functools

import jax
import jax.numpy as jnp
from jax import lax
from jax.experimental import pallas as pl
from jax.experimental.pallas import tpu as pltpu
from jax.sharding import PartitionSpec as P

NC = 64
NI = 128
ITERS = 3
f32 = jnp.float32
bf16 = jnp.bfloat16


def mm(a, b, dims=((1,), (0,))):
    return lax.dot_general(a, b, (dims, ((), ())), preferred_element_type=f32)


def split(x):
    high = x.astype(bf16)
    return high, (x - high.astype(f32)).astype(bf16)


def split_rows(x):
    high, low = split(x)
    return jnp.concatenate([high.astype(f32), low.astype(f32)], axis=0).astype(bf16)


def halves_dot(pair, x):
    n = pair.shape[0] // 2
    high, low = split(x)
    both = mm(pair, high)
    return both[0:n] + both[n:2 * n] + mm(pair[0:n], low)


def iota(shape, dim):
    return lax.broadcasted_iota(jnp.int32, shape, dim)


def kernel(
    n_sub, n_cl,
    s_hbm, loads_hbm, scale_hbm, basis_hbm, inv_hbm, weight_hbm, corner_hbm, iface_hbm, glue_hbm,
    out_ref,
    smat, loads_t, scale_ref, basis_ref, inv_ref, weight_ref, corner_ref, iface_ref, glue_ref,
    lv, nld, prd, nlz, prz, scol,
    b8, bt, dmat, zv, dv, xv, sv, qv,
    ohT, oh, ct, ctt, wide, invx, inv_own, grow, e_scr, ccol, wcol,
    st_src, st_buf,
    p1_src, p1_buf, rs_src, rs_buf, ag_src, ag_buf, p2_src, p2_buf, gl_src, gl_buf,
    tq, td, tz,
    load_sem, st_sem, p1_sem, rs_sem, ag_sem, p2_sem, gl_sem,
):
    me = lax.axis_index("sub")
    cl = lax.axis_index("cluster")
    r_cols, n_rows = loads_t.shape
    nz, cm = basis_ref.shape[0], inv_ref.shape[2]
    own = weight_ref.shape[1]
    half = own // 2
    nb = (n_rows - NC) // NI
    wst = st_src.shape[1]
    blk = 8 * n_sub

    barrier = pltpu.get_barrier_semaphore()

    @pl.loop(1, n_sub)
    def _(step):
        pl.semaphore_signal(barrier, inc=1, device_id={"sub": lax.rem(me + step, n_sub)})

    @pl.loop(1, n_cl)
    def _(step):
        pl.semaphore_signal(barrier, inc=1, device_id={"cluster": lax.rem(cl + step, n_cl)})

    fields = (
        (loads_hbm, loads_t), (basis_hbm, basis_ref), (scale_hbm, scale_ref), (inv_hbm, inv_ref),
        (corner_hbm, corner_ref), (weight_hbm, weight_ref), (iface_hbm, iface_ref),
        (glue_hbm, glue_ref), (s_hbm, smat),
    )
    copies = [pltpu.make_async_copy(a, b, load_sem.at[i]) for i, (a, b) in enumerate(fields)]
    for copy in copies:
        copy.start()

    def spread(src_of, buf, sem, axis, here, n, rows=8):
        @pl.loop(0, n - 1)
        def _(i):
            sign = 1 - 2 * lax.rem(i, 2)
            peer = lax.rem(here + n // 2 + sign * lax.div(i + 1, 2), n)
            pltpu.make_async_remote_copy(
                src_ref=src_of(peer).at[pl.ds(0, rows)],
                dst_ref=buf.at[here, pl.ds(0, rows)],
                send_sem=sem.at[0],
                recv_sem=sem.at[1],
                device_id={axis: peer},
            ).start()

    def drain(buf, sem, which, n, rows=8):
        view = buf.at[pl.ds(0, n - 1), pl.ds(0, rows)]
        pltpu.make_async_copy(view, view, sem.at[which]).wait()

    for copy in copies[:-1]:
        copy.wait()
    basis8 = jnp.concatenate([basis_ref[i] for i in range(nz)] + [jnp.zeros((8 - nz, n_rows), f32)], axis=0)
    b8[...] = split_rows(basis8)
    high, low = split(basis8)
    high, low = high.astype(f32), low.astype(f32)
    cols = jnp.transpose(
        jnp.concatenate([high, high, low, jnp.broadcast_to(scale_ref[...], (8, n_rows))], axis=0)
    )
    bt[...] = cols.astype(bf16)
    dmat[...] = jnp.broadcast_to(cols[:, 24:25], (n_rows, r_cols))

    corner_row = corner_ref[...]
    eye = iota((NC, NC), 0) == iota((NC, NC), 1)
    ccol[...] = jnp.sum(jnp.where(eye, corner_row, 0), axis=1, keepdims=True).astype(f32)
    corner_col = ccol[...].astype(jnp.int32)

    m = iota((blk, NC), 0)
    base = (m >> 3) * own + (m & 7)
    first, second = (base == corner_row).astype(f32), (base + half == corner_row).astype(f32)
    oh[...] = jnp.concatenate([first, second, first, second], axis=1).astype(bf16)
    m = iota((NC, blk), 1)
    base = (m >> 3) * own + (m & 7)
    pick = jnp.concatenate([base == corner_col, base + half == corner_col], axis=0)
    pick = pick.astype(f32).astype(bf16)
    ohT[...] = jnp.concatenate([pick, pick], axis=1)

    st_src[...] = jnp.zeros(st_src.shape, f32)
    for i in range(nz):
        st_src[i:i + 1, 0:cm] = inv_ref[i]
    st_src[0:nz, wst - NC:wst] = basis8[0:nz, 0:NC]
    st_src[nz:nz + 1, wst - NC:wst] = scale_ref[:, 0:NC]
    st_src[nz:nz + 1, NC:2 * NC] = corner_row.astype(f32)
    st_src[nz:nz + 1, 0:own] = weight_ref[...]

    ea, eb = iota((wst, blk), 0), iota((wst, blk), 1)
    grow[...] = (
        ((ea == (eb >> 3) * nz + (eb & 7)) & ((eb & 7) < nz) & (ea < cm)).astype(f32).astype(bf16)
    )
    row_ok = iota((8, wst), 0) < nz
    inv_own[...] = mm(split_rows(jnp.where(row_ok, st_src[...], 0.0)), grow[...]).astype(bf16)

    def packed_corners(v):
        zero = jnp.zeros((NC, r_cols), f32)
        parts = []
        for x in split(v):
            x = x.astype(f32)
            parts += [jnp.concatenate([x, zero], axis=1), jnp.concatenate([zero, x], axis=1)]
        return mm(oh[...], jnp.concatenate(parts, axis=0).astype(bf16))

    def basis_t(e):
        high, low = split(e)
        high, low = high.astype(f32), low.astype(f32)
        stack = jnp.concatenate([high, low, high, jnp.zeros((8, r_cols), f32)], axis=0)
        return mm(bt[...], stack.astype(bf16))

    tail = jnp.zeros((3, r_cols), f32)

    def first_message(k, vec, sums):
        pieces = halves_dot(b8[...], vec)
        sums = list(sums) + [jnp.zeros((1, r_cols), f32)] * (4 - len(sums))
        msg = jnp.concatenate(
            [
                jnp.concatenate([pieces[0:3], sums[0], sums[1], tail], axis=0),
                jnp.concatenate([pieces[3:6], sums[2], sums[3], tail], axis=0),
            ],
            axis=1,
        )
        p1_src[k] = msg
        p1_buf[k, me] = msg

    def send_first(k):
        spread(lambda peer: p1_src.at[k], p1_buf.at[k], p1_sem.at[k], "sub", me, n_sub, 5)

    def first_received(k):
        drain(p1_buf.at[k], p1_sem.at[k], 1, n_sub, 5)
        got = p1_buf[k]
        at = iota(got.shape, 1)
        got = jnp.where(at < 5, got, 0.0)
        moved = pltpu.roll(pltpu.roll(got, r_cols, 2), 3, 1)
        pieces = jnp.where(at < 3, got, jnp.where(at < nz, moved, 0.0))
        return pieces.reshape(blk, 2 * r_cols)[:, 0:r_cols], jnp.sum(got, axis=0)[3:5]

    def corner_message(k, vec):
        rs_src[k] = packed_corners(vec).reshape(n_sub, 8, 2 * r_cols)
        rs_buf[k, me] = rs_src[k, me]

    def send_corners(k):
        spread(lambda peer: rs_src.at[k, peer], rs_buf.at[k], rs_sem.at[k], "sub", me, n_sub)

    def own_corners(k):
        drain(rs_buf.at[k], rs_sem.at[k], 1, n_sub)
        total = jnp.sum(rs_buf[k], axis=0)
        ag_src[k] = total
        ag_buf[k, me] = total
        spread(lambda peer: ag_src.at[k], ag_buf.at[k], ag_sem.at[k], "sub", me, n_sub)

    def corner_back(k):
        drain(ag_buf.at[k], ag_sem.at[k], 1, n_sub)
        got = ag_buf[k].reshape(blk, 2 * r_cols)
        high, low = split(got)
        quad = mm(ohT[...], jnp.concatenate([high, low], axis=0))
        return quad[0:NC, 0:r_cols] + quad[NC:2 * NC, r_cols:2 * r_cols]

    glue_here = glue_ref[...].astype(f32)
    hi = NI // 2

    def placed(side, b):
        return (iface_ref[0:1, 1 - side:2 - side] == b).astype(f32)

    def block_of(side, ref):
        rows = jnp.zeros((NI, r_cols), f32)
        for b in range(nb):
            rows = rows + placed(side, b) * ref[NC + b * NI:NC + (b + 1) * NI, :]
        return rows

    def send_glue(k, ref):
        for side in range(2):
            rows = block_of(side, ref)
            gl_src[k, side, 0:hi, :] = jnp.concatenate([rows[0:hi], rows[hi:NI]], axis=1)
            gl_src[k, side, hi:hi + 8, :] = jnp.broadcast_to(glue_here, (8, 2 * r_cols))
        for side, peer in ((0, lax.rem(cl + 1, n_cl)), (1, lax.rem(cl + n_cl - 1, n_cl))):
            pltpu.make_async_remote_copy(
                src_ref=gl_src.at[k, side],
                dst_ref=gl_buf.at[k, side],
                send_sem=gl_sem.at[k, side, 0],
                recv_sem=gl_sem.at[k, side, 1],
                device_id={"cluster": peer},
            ).start()

    def glue_wait(k, which):
        for side in range(2):
            pltpu.make_async_copy(
                gl_src.at[k, side], gl_buf.at[k, side], gl_sem.at[k, side, which]
            ).wait()

    def unpack(k, side):
        a = gl_buf[k, side, 0:hi, :]
        return jnp.concatenate([a[:, 0:r_cols], a[:, r_cols:2 * r_cols]], axis=0)

    def spread_static():
        @pl.loop(1, n_sub // 2)
        def _(i):
            pltpu.make_async_remote_copy(
                src_ref=st_src.at[pl.ds(0, 7)],
                dst_ref=st_buf.at[core, place, pl.ds(0, 7)],
                send_sem=st_sem.at[0],
                recv_sem=st_sem.at[1],
                device_id={"sub": lax.rem(me + 2 * i, n_sub)},
            ).start()

    def pair_static():
        view = st_buf.at[0, pl.ds(0, n_sub // 2 - 1), pl.ds(0, 7)]
        pltpu.make_async_copy(view, view, st_sem.at[1]).wait()
        pltpu.make_async_remote_copy(
            src_ref=st_buf.at[core, :, pl.ds(0, 7)],
            dst_ref=st_buf.at[core, :, pl.ds(0, 7)],
            send_sem=st_sem.at[2],
            recv_sem=st_sem.at[3],
            device_id={"sub": me + 1 - 2 * core},
        ).start()

    lv[...] = jnp.transpose(loads_t[...])
    loads = lv[...]
    scaled = dmat[...] * loads
    corner_message(0, scaled[0:NC, :])
    first_message(0, loads, [jnp.sum(scaled * loads, axis=0, keepdims=True)])
    core, place = lax.rem(me, 2), lax.div(me, 2)
    st_buf[core, place] = st_src[...]

    pl.semaphore_wait(barrier, n_sub + n_cl - 2)

    send_corners(0)
    send_first(0)
    spread_static()
    copies[-1].wait()
    own_corners(0)
    first_pieces, first_sums = first_received(0)
    z = dmat[...] * lv[...] + basis_t(halves_dot(inv_own[...], first_pieces))
    zv[...] = z
    dv[...] = z

    def jumps(k, step, beta):
        glue_wait(k, 1)
        if k == 0:
            nlz[...] = unpack(k, 1)
            prz[...] = unpack(k, 0)
            nld[...] = nlz[...]
            prd[...] = prz[...]
        else:
            nlz[...] = nlz[...] - step * unpack(k, 1)
            prz[...] = prz[...] - step * unpack(k, 0)
            nld[...] = nlz[...] + beta * nld[...]
            prd[...] = prz[...] + beta * prd[...]
        prev_glue = gl_buf[0, 0, hi:hi + 1, 0:r_cols]
        return glue_here * (block_of(0, dv) - nld[...]), prev_glue * (prd[...] - block_of(1, dv))

    def add_jumps(jump):
        for b in range(nb):
            rows = slice(NC + b * NI, NC + (b + 1) * NI)
            sv[rows, :] = sv[rows, :] + placed(0, b) * jump[0] - placed(1, b) * jump[1]

    def product(k, last, step, beta):
        half_d = dv[...].astype(bf16)
        top = mm(smat[0:NC, :], half_d)
        sv[0:NC, :] = top
        if not last:
            corner_message(k + 1, dmat[0:NC, :] * top)
        if k == 0:
            send_glue(0, zv)
        elif not last:
            send_corners(k + 1)
        if k > 0:
            jump = jumps(k, step, beta)
        sv[NC:, :] = mm(smat[NC:, :], half_d)
        if k > 0:
            add_jumps(jump)

    product(0, False, None, None)

    lane = iota((NC, NC), 1).astype(f32)
    row_ok = (iota((8, wst), 0) < nz) & (iota((8, wst), 1) < cm)
    tile_ok = iota((8, NC), 0) <= nz
    n_half = n_sub // 2

    def tables(side, ws, srow):
        stack = []
        for i in range(n_half):
            slot = st_buf[side, i]
            tile = jnp.where(tile_ok, slot[:, wst - NC:wst], 0.0)
            match = (ccol[...] == slot[nz:nz + 1, NC:2 * NC]).astype(f32).astype(bf16)
            both = mm(split_rows(tile), match, ((1,), (1,)))
            rows = both[0:8] + both[8:16]
            s = 2 * i + side
            ct[pl.ds(pl.multiple_of(8 * s, 8), 8), :] = rows
            srow = srow + rows[nz:nz + 1, :]
            mine = (ccol[...] - (s * own).astype(f32) == lane) & (lane < own)
            ws = ws + jnp.where(mine, slot[nz:nz + 1, 0:NC], 0.0)
            stack.append(jnp.where(row_ok, slot, 0.0))
        both = mm(split_rows(jnp.concatenate(stack, axis=0)), grow[...])
        for i in range(n_half):
            row = pl.multiple_of(8 * (2 * i + side), 8)
            wide[pl.ds(row, 8), :] = both[8 * i:8 * i + 8]
            wide[pl.ds(blk + row, 8), :] = both[8 * (n_half + i):8 * (n_half + i) + 8]
        return ws, srow

    pair_static()
    send_corners(1)
    ws, srow = tables(core, jnp.zeros((NC, NC), f32), jnp.zeros((1, NC), f32))
    view = st_buf.at[0, :, pl.ds(0, 7)]
    pltpu.make_async_copy(view, view, st_sem.at[3]).wait()
    ws, srow = tables(1 - core, ws, srow)
    wcol[...] = jnp.sum(ws, axis=1, keepdims=True)
    scol[...] = jnp.sum(jnp.where(eye, srow, 0.0), axis=1, keepdims=True) * wcol[...]
    ctt[...] = split_rows(jnp.transpose(ct[...]))
    invx[...] = wide[...].astype(bf16)

    def coarse(pieces):
        e_all = halves_dot(invx[...], pieces)
        e_scr[...] = e_all
        return jnp.sum(pieces * e_all, axis=0, keepdims=True)

    rho_part = first_sums[0:1, 0:r_cols] + coarse(first_pieces)
    tz[...] = corner_back(0) + halves_dot(ctt[...], e_scr[...])
    td[...] = tz[...]
    xv[...] = jnp.zeros_like(xv)

    rho = step = beta = None
    for k in range(ITERS):
        last = k + 1 == ITERS
        sv[0:NC, :] = sv[0:NC, :] + wcol[...] * td[...]
        if k == 0:
            add_jumps(jumps(0, None, None))
        s, d = sv[...], dv[...]
        curve_part = jnp.sum(d * s, axis=0, keepdims=True)
        if not last:
            ds = dmat[...] * s
            sums = [
                curve_part,
                jnp.sum(zv[...] * s, axis=0, keepdims=True),
                jnp.sum(ds * s, axis=0, keepdims=True),
            ]
            first_message(k + 1, s, sums)
            send_first(k + 1)
            own_corners(k + 1)
            pieces, sums = first_received(k + 1)
            quad = coarse(pieces)
            parts = [sums[0:1, 0:r_cols], sums[1:2, 0:r_cols], sums[0:1, r_cols:] + quad]
        else:
            msg = jnp.concatenate([curve_part, curve_part], axis=1)
            p1_src[k + 1, 0:1] = msg
            p1_buf[k + 1, me, 0:1] = msg
            spread(lambda peer: p1_src.at[k + 1], p1_buf.at[k + 1], p1_sem.at[k + 1],
                   "sub", me, n_sub, 1)
            drain(p1_buf.at[k + 1], p1_sem.at[k + 1], 1, n_sub, 1)
            sums = jnp.sum(p1_buf[k + 1, :, 0:1], axis=0)[:, 0:r_cols]
            parts = [sums, sums, sums]
        msg = jnp.concatenate(
            [
                jnp.concatenate([parts[0], parts[1]], axis=1),
                jnp.concatenate([parts[2], rho_part], axis=1),
            ],
            axis=0,
        )
        p2_src[k] = msg
        p2_buf[k, cl] = msg
        spread(lambda peer: p2_src.at[k], p2_buf.at[k], p2_sem.at[k], "cluster", cl, n_cl, 2)
        if not last:
            e_own = e_scr[pl.ds(8 * me, 8), :]
            qv[...] = ds + basis_t(e_own)
            send_glue(k + 1, qv)
            tq[...] = scol[...] * td[...] + halves_dot(ctt[...], e_scr[...])
        else:
            loads_t[...] = jnp.transpose(xv[...])
            out_ref[...] = jnp.transpose(dv[...])
        drain(p2_buf.at[k], p2_sem.at[k], 1, n_cl, 2)
        total = jnp.sum(p2_buf[k], axis=0)
        curve = total[0:1, 0:r_cols]
        if k == 0:
            rho = total[1:2, r_cols:2 * r_cols]
        step = rho / curve
        if last:
            same = iota((r_cols, r_cols), 0) == iota((r_cols, r_cols), 1)
            step = jnp.sum(jnp.where(same, step, 0.0), axis=1, keepdims=True)
            out_ref[...] = loads_t[...] + step * out_ref[...]
            break
        zs = total[0:1, r_cols:2 * r_cols]
        sq = total[1:2, 0:r_cols]
        rho_next = rho - 2.0 * step * zs + step * (step * sq)
        beta = rho_next / rho
        d = dv[...]
        z = zv[...] - step * qv[...]
        zv[...] = z
        dv[...] = z + beta * d
        xv[...] = xv[...] + step * d
        rho = rho_next
        product(k + 1, k + 2 == ITERS, step, beta)
        tz[...] = tz[...] - step * (tq[...] + corner_back(k + 1))
        td[...] = tz[...] + beta * td[...]

    view = st_buf.at[0, pl.ds(0, n_sub // 2 - 1), pl.ds(0, 7)]
    pltpu.make_async_copy(view, view, st_sem.at[0]).wait()
    view = st_buf.at[0, :, pl.ds(0, 7)]
    pltpu.make_async_copy(view, view, st_sem.at[2]).wait()
    for k in range(ITERS + 1):
        drain(p1_buf.at[k], p1_sem.at[k], 0, n_sub, 5 if k < ITERS else 1)
    for k in range(ITERS):
        drain(rs_buf.at[k], rs_sem.at[k], 0, n_sub)
        drain(ag_buf.at[k], ag_sem.at[k], 0, n_sub)
        drain(p2_buf.at[k], p2_sem.at[k], 0, n_cl, 2)
        glue_wait(k, 0)


def per_device(
    n_sub, n_cl, schur_block, load_cases, precond_scale, coarse_basis, coarse_inverse,
    corner_weight, corner_index, iface_block, glue_link,
):
    n_rows, r = load_cases.shape[2:]
    nz, cm = coarse_basis.shape[2], coarse_inverse.shape[2]
    blk = 8 * n_sub
    wst = max(-(-(cm + NC) // 128) * 128, 4 * NC)
    vec = pltpu.VMEM((n_rows, r), f32)
    vmem = pl.BlockSpec(memory_space=pltpu.VMEM)
    hbm = pl.BlockSpec(memory_space=pltpu.HBM)
    own = corner_weight.shape[1]
    dma = pltpu.SemaphoreType.DMA
    operands = (
        schur_block[0, 0], load_cases[0, 0].T, precond_scale[0],
        jnp.swapaxes(coarse_basis[0], 0, 1), jnp.swapaxes(coarse_inverse, 0, 1),
        corner_weight, corner_index[0], iface_block[0],
    )
    out = pl.pallas_call(
        functools.partial(kernel, n_sub, n_cl),
        out_shape=jax.ShapeDtypeStruct((r, n_rows), f32),
        in_specs=[hbm] * 9,
        out_specs=vmem,
        scratch_shapes=[
            pltpu.VMEM((n_rows, n_rows), bf16),
            pltpu.VMEM((r, n_rows), f32),
            pltpu.VMEM((1, n_rows), f32),
            pltpu.VMEM((nz, 1, n_rows), f32),
            pltpu.VMEM((nz, 1, cm), f32),
            pltpu.VMEM((1, own), f32),
            pltpu.VMEM((1, NC), jnp.int32),
            pltpu.VMEM((1, 2), jnp.int32),
            pltpu.VMEM((1, 1), jnp.int32),
            vec,
            pltpu.VMEM((NI, r), f32),
            pltpu.VMEM((NI, r), f32),
            pltpu.VMEM((NI, r), f32),
            pltpu.VMEM((NI, r), f32),
            pltpu.VMEM((NC, 1), f32),
            pltpu.VMEM((16, n_rows), bf16),
            pltpu.VMEM((n_rows, 32), bf16),
            vec, vec, vec, vec, vec, vec,
            pltpu.VMEM((2 * NC, 2 * blk), bf16),
            pltpu.VMEM((blk, 4 * NC), bf16),
            pltpu.VMEM((blk, NC), f32),
            pltpu.VMEM((2 * NC, blk), bf16),
            pltpu.VMEM((2 * blk, blk), f32),
            pltpu.VMEM((2 * blk, blk), bf16),
            pltpu.VMEM((16, blk), bf16),
            pltpu.VMEM((wst, blk), bf16),
            pltpu.VMEM((blk, r), f32),
            pltpu.VMEM((NC, 1), f32),
            pltpu.VMEM((NC, 1), f32),
            pltpu.VMEM((8, wst), f32),
            pltpu.VMEM((2, n_sub // 2, 8, wst), f32),
            pltpu.VMEM((ITERS + 1, 8, 2 * r), f32),
            pltpu.VMEM((ITERS + 1, n_sub, 8, 2 * r), f32),
            pltpu.VMEM((ITERS, n_sub, 8, 2 * r), f32),
            pltpu.VMEM((ITERS, n_sub, 8, 2 * r), f32),
            pltpu.VMEM((ITERS, 8, 2 * r), f32),
            pltpu.VMEM((ITERS, n_sub, 8, 2 * r), f32),
            pltpu.VMEM((ITERS, 2, 2 * r), f32),
            pltpu.VMEM((ITERS, n_cl, 2, 2 * r), f32),
            pltpu.VMEM((ITERS, 2, NI // 2 + 8, 2 * r), f32),
            pltpu.VMEM((ITERS, 2, NI // 2 + 8, 2 * r), f32),
            pltpu.VMEM((NC, r), f32),
            pltpu.VMEM((NC, r), f32),
            pltpu.VMEM((NC, r), f32),
            dma((9,)),
            dma((4,)),
            dma((ITERS + 1, 2)),
            dma((ITERS, 2)),
            dma((ITERS, 2)),
            dma((ITERS, 2)),
            dma((ITERS, 2, 2)),
        ],
        compiler_params=pltpu.CompilerParams(
            collective_id=0, has_side_effects=True, vmem_limit_bytes=40 * 1024 * 1024
        ),
    )(
        *(pltpu.with_memory_space_constraint(a, pltpu.HBM) for a in operands), glue_link,
    )
    return out.T[None, None]


def solution(mesh):
    in_specs = (
        P("cluster", "sub", None, None),
        P("cluster", "sub", None, None),
        P("cluster", "sub", None),
        P("cluster", "sub", None, None),
        P("cluster", "sub", None),
        P("cluster", "sub"),
        P("cluster", "sub", None),
        P("cluster", "sub", None),
        P("cluster", "sub"),
    )
    return jax.shard_map(
        functools.partial(per_device, mesh.shape["sub"], mesh.shape["cluster"]),
        mesh=mesh, in_specs=in_specs, out_specs=P("cluster", "sub", None, None), check_vma=False,
    )
```
